512 devices in a mesh: runs: 64 (over x, z), tm: 8 (over y, core).
Axes of the slice: x: 4, y: 4, z: 16, core: 2. Of those that a mesh axis runs over, the one named last changes fastest.
Arguments:
- tensor: bfloat16 [1024, 128, 1024], P('runs', 'tm'), may hold values from 0 to 1
- run_counts: int32 [64], P('runs'), may hold values from 4 to 16, as said below
- run_init: float32 [1024, 128], P('runs'), may hold values from 0.05 to 0.5
- bin_init: float32 [1024, 128], replicated, may hold values from 0.05 to 0.5
- time_init: float32 [128, 128], P('tm'), may hold values from 0.05 to 0.5
Outputs:
- run_factor: float32 [1024, 128], P('runs')
- bin_factor: float32 [1024, 128], replicated
- time_factor: float32 [128, 128], P('tm')
The draws below stay inside these ranges and needn't reach their ends.
Inputs may be any that keep to these rules, and one draw needn't show every extreme that they name: `run_counts`: at most 16 live slots on an index of runs; some index has exactly 16.
All inputs are finite; a program needn't handle non-finite values.
Results may differ from the reference program's by a relative error of at most 0.0003.
Values sent between devices are 32-bit elements; how exact they have to be, the bound alone decides.
No kernel may reach another device: no remote copies, remote signals or barrier semaphores. Data moves between devices by JAX's collectives and lax.ppermute only.
A program may use at most 64 MiB of HBM per device.

```python
import math
import jax
import jax.numpy as jnp
from jax import lax

ROWCAP = 16
J = 1024
R = 128
OUTER = 1
INNER = 1
RUNS_CAP = 1024
TIMES = 128
N_RUNS = 64


def draw_run_counts(key, part):
    first = jax.random.fold_in(key, 11)
    second = jax.random.fold_in(key, 23)
    counts = jax.random.randint(first, (N_RUNS,), ROWCAP // 4, ROWCAP // 2 + 1)
    peak = jax.random.randint(second, (), 0, N_RUNS)
    position = jnp.arange(N_RUNS, dtype=jnp.int32)
    return jnp.where(position == peak, ROWCAP, counts).astype(jnp.int32)


def log_uniform(key, shape, lower, upper):
    exponent = jax.random.uniform(key, shape, jnp.float32, jnp.log(lower), jnp.log(upper))
    return jnp.exp(exponent)


def draw_tensor(key, part):
    components = 5 * R // 4
    run_key = jax.random.fold_in(key, 101)
    time_key = jax.random.fold_in(key, 103)
    centre_key = jax.random.fold_in(key, 104)
    breadth_key = jax.random.fold_in(key, 105)
    rough_key = jax.random.fold_in(key, 106)
    noise_key = jax.random.fold_in(key, 107)
    run_load = log_uniform(run_key, (RUNS_CAP, components), 0.02, 1.0)
    time_load = log_uniform(time_key, (TIMES, components), 0.02, 1.0)
    spread = 0.15
    divisor = 0.08 * components
    centre = jax.random.uniform(centre_key, (components,), jnp.float32, 0.0, 1.0)
    breadth = jax.random.uniform(breadth_key, (components,), jnp.float32, 0.05, 0.25)
    position = (jnp.arange(J, dtype=jnp.float32) + 0.5) / J
    profile = jnp.exp(-0.5 * ((position[:, None] - centre[None, :]) / breadth[None, :]) ** 2)
    roughness = jax.random.uniform(rough_key, (J, components), jnp.float32, 0.5, 1.5)
    spectra = (0.1 + profile) * roughness

    def single_run(index):
        loadings = time_load * run_load[index][None, :]
        signal = jnp.dot(loadings, spectra.T, precision=lax.Precision.HIGHEST)
        noise = jax.random.uniform(jax.random.fold_in(noise_key, index), (TIMES, J), jnp.float32, 1.0 - spread, 1.0 + spread)
        return jnp.clip(signal * noise / divisor, 0.0, 1.0)
    return lax.map(single_run, jnp.arange(RUNS_CAP, dtype=jnp.int32)).astype(jnp.bfloat16)


def level_of(stream_key, extent, shards, least, largest):
    gain = 1.0
    for dim, blocks in shards:
        heights = jax.random.uniform(jax.random.fold_in(jax.random.fold_in(stream_key, 6), dim), (blocks,), jnp.float32, least / len(shards), largest / len(shards))
        gain = gain * jnp.repeat(jnp.exp(heights), extent[dim] // blocks).reshape((-1,) + (1,) * (len(extent) - 1 - dim))
    return gain


def setup_inputs(seed: int = 0) -> dict:
    arg_keys = jax.random.split(jax.random.key(seed), 6)
    return {
        "tensor": draw_tensor(jax.random.fold_in(arg_keys[5], 71), 0),
        "run_counts": draw_run_counts(jax.random.fold_in(arg_keys[5], 71), 0),
        "run_init": jnp.clip(jnp.exp(math.log(0.5) - 2.3025851 * jax.random.uniform(arg_keys[2], (RUNS_CAP, R), jnp.float32) ** level_of(arg_keys[2], (RUNS_CAP, R), ((0, 64),), -0.2, 0.2)), 0.05, 0.5),
        "bin_init": jnp.clip(jnp.exp(jax.random.uniform(arg_keys[3], (J, R), jnp.float32, math.log(0.05), math.log(0.5))), 0.05, 0.5),
        "time_init": jnp.clip(jnp.exp(math.log(0.5) - 2.3025851 * jax.random.uniform(arg_keys[4], (TIMES, R), jnp.float32) ** level_of(arg_keys[4], (TIMES, R), ((0, 8),), -0.2, 0.2)), 0.05, 0.5),
    }


HIGH = lax.Precision.HIGHEST


def low(factor):
    return lax.optimization_barrier(factor.astype(jnp.bfloat16)).astype(jnp.float32)


def gram(factor):
    return jnp.dot(factor.T, factor, precision=HIGH)


def reference(tensor, run_counts, run_init, bin_init, time_init):
    slot = jnp.arange(RUNS_CAP, dtype=jnp.int32)
    owner = slot // ROWCAP
    live = ((slot % ROWCAP) < run_counts[owner]).astype(jnp.float32)[:, None]
    slabs = tensor.reshape(N_RUNS, ROWCAP, TIMES, J)
    runs = run_init * live
    bins = bin_init
    times = time_init
    run_gram = gram(runs)
    bin_gram = gram(bins)
    time_gram = gram(times)

    def bin_contract(bins_now):
        bins_low = low(bins_now)

        def one(slab):
            return jnp.einsum('ikj,jr->ikr', slab.astype(jnp.float32), bins_low, precision=HIGH)

        return lax.map(one, slabs).reshape(RUNS_CAP, TIMES, R)

    for outer in range(OUTER):
        for inner in range(INNER):
            inner_sum = bin_contract(bins)
            time_terms = jnp.einsum('ir,ikr->kr', runs, inner_sum, precision=HIGH)
            times = times * time_terms / jnp.dot(times, run_gram * bin_gram, precision=HIGH)
            time_gram = gram(times)
            times_low = low(times)
            run_slabs = runs.reshape(N_RUNS, ROWCAP, R)

            def bin_piece(pair):
                slab, rows = pair
                partial_value = jnp.einsum('ikj,kr->ijr', slab.astype(jnp.float32), times_low, precision=HIGH)
                return jnp.einsum('ir,ijr->jr', rows, partial_value, precision=HIGH)

            bin_terms = jnp.sum(lax.map(bin_piece, (slabs, run_slabs)), axis=0)
            bins = bins * bin_terms / jnp.dot(bins, run_gram * time_gram, precision=HIGH)
            bin_gram = gram(bins)
        inner_sum = bin_contract(bins)
        run_terms = jnp.einsum('kr,ikr->ir', times, inner_sum, precision=HIGH)
        runs = runs * run_terms / (jnp.dot(runs, bin_gram * time_gram, precision=HIGH) + 1.0 - live)
        run_gram = gram(runs)
    return runs, bins, times
```

```python
import jax
import jax.numpy as jnp
from jax import lax
from jax.sharding import Mesh, PartitionSpec as P

HIGH = lax.Precision.HIGHEST
F32 = jnp.float32
BF16 = jnp.bfloat16
SIZES = {"x": 4, "z": 16, "y": 4, "c": 2}
PLANE = ("x", "y", "c")
TM = ("y", "c")


def gram(factor):
    return jnp.dot(factor.T, factor, precision=HIGH)


def extent(axes):
    total = 1
    for axis in axes:
        total *= SIZES[axis]
    return total


def exchange(parts, axes):
    return lax.all_to_all(parts, axes, 0, 0)


def spread(value, axes):
    copies = jnp.broadcast_to(value[None], (extent(axes),) + value.shape)
    return exchange(copies, axes)


def total(value, axes):
    return jnp.sum(spread(value, axes), axis=0)


def pieces(value):
    out = []
    for _ in range(3):
        part = lax.reduce_precision(value, 8, 7)
        out.append(part.astype(BF16))
        value = value - part
    return out


def shards(tensor, run_counts, run_init, bin_init, time_init):
    rowcap, rows, width = tensor.shape
    rank = run_init.shape[1]
    live = (jnp.arange(rowcap, dtype=jnp.int32) < run_counts[0]).astype(F32)[:, None]
    flat = tensor.reshape(rowcap * rows, width)
    runs = run_init * live
    bins_t = bin_init.T
    times = time_init

    run_gram = gram(runs)
    bin_gram = gram(bin_init)
    inner = jnp.dot(flat, bin_init.astype(BF16), preferred_element_type=F32)
    terms = jnp.sum(runs[:, None, :] * inner.reshape(rowcap, rows, rank), axis=0)
    below = jnp.dot(times, run_gram * bin_gram, precision=HIGH)
    both = jnp.concatenate([terms, below], axis=0)
    both = total(total(both, ("x",)), ("z",))
    times = times * both[:rows] / both[rows:]

    low = times.astype(BF16).astype(F32)
    weights = (runs[:, None, :] * low[None, :, :]).reshape(rowcap * rows, rank)
    terms = sum(
        lax.dot_general(part, flat, (((0,), (0,)), ((), ())), preferred_element_type=F32)
        for part in pieces(weights)
    )
    time_gram = gram(times)
    both = jnp.concatenate([terms, run_gram * time_gram], axis=1)
    count = extent(PLANE)
    chunk = rank // count
    both = jnp.sum(exchange(both.reshape(count, chunk, width + rank), PLANE), axis=0)
    both = total(both, ("z",))
    below = jnp.dot(both[:, width:], bins_t, precision=HIGH)
    mine = lax.dynamic_slice_in_dim(bins_t, lax.axis_index(PLANE) * chunk, chunk, 0)
    mine = mine * both[:, :width] / below
    bins_t = spread(mine, PLANE).reshape(rank, width)

    inner = lax.dot_general(
        flat, bins_t.astype(BF16), (((1,), (1,)), ((), ())), preferred_element_type=F32
    )
    terms = jnp.sum(times[None, :, :] * inner.reshape(rowcap, rows, rank), axis=1)
    bin_gram = jnp.dot(bins_t, bins_t.T, precision=HIGH)
    below = jnp.dot(runs, bin_gram * time_gram, precision=HIGH)
    both = total(jnp.concatenate([terms, below], axis=0), TM)
    runs = runs * both[:rowcap] / (both[rowcap:] + 1.0 - live)
    return (runs, bins_t.T, times)


def solution(mesh):
    fine = Mesh(mesh.devices.reshape(tuple(SIZES.values())), tuple(SIZES))
    return jax.shard_map(
        shards,
        mesh=fine,
        in_specs=(P(("x", "z"), TM, None), P(("x", "z")), P(("x", "z"), None), P(), P(TM, None)),
        out_specs=(P(("x", "z"), None), P(), P(TM, None)),
        check_vma=False,
    )
```

```python
import jax
import jax.numpy as jnp
from jax import lax
from jax.sharding import Mesh, PartitionSpec as P

HIGH = lax.Precision.HIGHEST
F32 = jnp.float32
BF16 = jnp.bfloat16
SIZES = {"x": 4, "h": 8, "l": 2, "y": 4, "c": 2}
RUNS = ("x", "h", "l")
NEAR = ("x", "l")
FAR = ("h",)
PLANE = ("x", "l", "y", "c")
TM = ("y", "c")


def gram(factor):
    return jnp.dot(factor.T, factor, precision=HIGH)


def extent(axes):
    total = 1
    for axis in axes:
        total *= SIZES[axis]
    return total


def exchange(parts, axes):
    return lax.all_to_all(parts, axes, 0, 0)


def spread(value, axes):
    copies = jnp.broadcast_to(value[None], (extent(axes),) + value.shape)
    return exchange(copies, axes)


def total(value, axes):
    return jnp.sum(spread(value, axes), axis=0)


def pieces(value):
    out = []
    for _ in range(3):
        part = lax.reduce_precision(value, 8, 7)
        out.append(part.astype(BF16))
        value = value - part
    return out


def shards(tensor, run_counts, run_init, bin_init, time_init):
    rowcap, rows, width = tensor.shape
    rank = run_init.shape[1]
    live = (jnp.arange(rowcap, dtype=jnp.int32) < run_counts[0]).astype(F32)[:, None]
    flat = tensor.reshape(rowcap * rows, width)
    runs = run_init * live
    bins_t = bin_init.T
    times = time_init

    run_gram = gram(runs)
    bin_gram = gram(bin_init)
    inner = jnp.dot(flat, bin_init.astype(BF16), preferred_element_type=F32)
    terms = jnp.sum(runs[:, None, :] * inner.reshape(rowcap, rows, rank), axis=0)
    below = jnp.dot(times, run_gram * bin_gram, precision=HIGH)
    both = jnp.concatenate([terms, below], axis=0)
    both = total(total(both, NEAR), FAR)
    times = times * both[:rows] / both[rows:]

    low = lax.reduce_precision(times, 8, 7)
    weights = (runs[:, None, :] * low[None, :, :]).reshape(rowcap * rows, rank)
    terms = sum(
        lax.dot_general(part, flat, (((0,), (0,)), ((), ())), preferred_element_type=F32)
        for part in pieces(weights)
    )
    time_gram = gram(times)
    both = jnp.concatenate([terms, run_gram * time_gram], axis=1)
    count = extent(PLANE)
    chunk = rank // count
    both = jnp.sum(exchange(both.reshape(count, chunk, width + rank), PLANE), axis=0)
    both = total(both, FAR)
    below = jnp.dot(both[:, width:], bins_t, precision=HIGH)
    mine = lax.dynamic_slice_in_dim(bins_t, lax.axis_index(PLANE) * chunk, chunk, 0)
    mine = mine * both[:, :width] / below
    bins_t = spread(mine, PLANE).reshape(rank, width)

    inner = lax.dot_general(
        flat, bins_t.astype(BF16), (((1,), (1,)), ((), ())), preferred_element_type=F32
    )
    terms = jnp.sum(times[None, :, :] * inner.reshape(rowcap, rows, rank), axis=1)
    bin_gram = jnp.dot(bins_t, bins_t.T, precision=HIGH)
    below = jnp.dot(runs, bin_gram * time_gram, precision=HIGH)
    both = total(jnp.concatenate([terms, below], axis=0), TM)
    runs = runs * both[:rowcap] / (both[rowcap:] + 1.0 - live)
    return (runs, bins_t.T, times)


def solution(mesh):
    fine = Mesh(mesh.devices.reshape(tuple(SIZES.values())), tuple(SIZES))
    return jax.shard_map(
        shards,
        mesh=fine,
        in_specs=(P(RUNS, TM, None), P(RUNS), P(RUNS, None), P(), P(TM, None)),
        out_specs=(P(RUNS, None), P(), P(TM, None)),
        check_vma=False,
    )
```

```python
import jax
import jax.numpy as jnp
from jax import lax
from jax.experimental import pallas as pl
from jax.experimental.pallas import tpu as pltpu
from jax.sharding import Mesh, PartitionSpec as P

HIGH = lax.Precision.HIGHEST
F32 = jnp.float32
BF16 = jnp.bfloat16
SIZES = {"x": 4, "h": 8, "l": 2, "y": 4, "c": 2}
RUNS = ("x", "h", "l")
NEAR = ("x", "l")
FAR = ("h",)
PLANE = ("x", "l", "y", "c")
TM = ("y", "c")
FIRST = (((0,), (0,)), ((), ()))
LAST = (((1,), (1,)), ((), ()))


def exact(left, right, dims):
    return lax.dot_general(left, right, dims, precision=HIGH, preferred_element_type=F32)


def quick(left, right, dims):
    return lax.dot_general(left, right, dims, preferred_element_type=F32)


def extent(axes):
    total = 1
    for axis in axes:
        total *= SIZES[axis]
    return total


def exchange(parts, axes):
    return lax.all_to_all(parts, axes, 0, 0)


def added(parts):
    total = parts[0]
    for part in range(1, parts.shape[0]):
        total += parts[part]
    return total


def terms_kernel(count, index, *refs):
    far, (both, runs_out, gram_out, pick, *near), sems = refs[:4], refs[4:12], refs[12]
    tensor, bins, run_init, times = near
    copies = [pltpu.make_async_copy(far[i], near[i], sems.at[i]) for i in range(4)]
    for copy in reversed(copies):
        copy.start()
    rowcap, rank = run_init.shape
    rows = times.shape[0]
    chunk = pick.shape[0]
    row = lax.broadcasted_iota(jnp.int32, (chunk, rank), 0) + index[0] * chunk
    column = lax.broadcasted_iota(jnp.int32, (chunk, rank), 1)
    pick[...] = jnp.where(column == row, 1.0, 0.0)
    slot = lax.broadcasted_iota(jnp.int32, (rowcap, rank), 0)
    copies[2].wait()
    copies[3].wait()
    runs = jnp.where(slot < count[0], run_init[...], 0.0)
    runs_out[...] = runs
    run_gram = exact(runs, runs, FIRST)
    gram_out[...] = run_gram
    copies[1].wait()
    full = bins[...]
    below = jnp.dot(times[...], run_gram * exact(full, full, FIRST), precision=HIGH)
    copies[0].wait()
    inner = jnp.dot(tensor[...], full.astype(BF16), preferred_element_type=F32)
    terms = runs[0:1] * inner[0:rows]
    for i in range(1, rowcap):
        terms += runs[i : i + 1] * inner[i * rows : (i + 1) * rows]
    for copy in range(both.shape[0]):
        both[copy, 0:rows] = terms
        both[copy, rows:] = below


def time_kernel(parts, times, runs, run_gram, tensor, out, times_out, gram_out):
    rows, rank = times.shape
    rowcap = runs.shape[0]
    width = tensor.shape[1]
    sums = added(parts)
    new = times[...] * sums[:rows] / sums[rows:]
    times_out[...] = new
    time_gram = exact(new, new, FIRST)
    gram_out[...] = time_gram
    low = new.astype(BF16).astype(F32)
    left = jnp.concatenate([runs[i : i + 1] * low for i in range(rowcap)], axis=0)
    block = tensor[...]
    terms = None
    for _ in range(3):
        part = left.astype(BF16)
        term = quick(part, block, FIRST)
        terms = term if terms is None else terms + term
        left = left - part.astype(F32)
    out[:, :, 0:width] = terms.reshape(out.shape[0], out.shape[1], width)
    mixing = run_gram[...] * time_gram
    out[:, :, width:] = mixing.reshape(out.shape[0], out.shape[1], rank)


def spread_kernel(parts, out):
    total = added(parts)
    for copy in range(out.shape[0]):
        out[copy] = total


def bins_kernel(parts, bins, pick, out):
    count, chunk, width = out.shape
    sums = added(parts)
    left = jnp.concatenate([sums[:, width:], pick[...]], axis=0)
    got = exact(left, bins[...], LAST)
    mine = got[chunk:] * sums[:, :width] / got[:chunk]
    for copy in range(count):
        out[copy] = mine


def runs_kernel(parts, tensor, runs, times, time_gram, both, bins_out):
    rank, width = bins_out.shape
    rowcap = runs.shape[0]
    rows = times.shape[0]
    bins = parts[...].reshape(rank, width)
    bins_out[...] = bins
    inner = quick(tensor[...], bins.astype(BF16), LAST)
    mixing = exact(bins, bins, LAST) * time_gram[...]
    below = jnp.dot(runs[...], mixing, precision=HIGH)
    for copy in range(both.shape[0]):
        both[copy, rowcap:] = below
    for i in range(rowcap):
        term = jnp.sum(times[...] * inner[i * rows : (i + 1) * rows], axis=0, keepdims=True)
        for copy in range(both.shape[0]):
            both[copy, i : i + 1] = term


def last_kernel(count, parts, runs, out):
    rowcap, rank = runs.shape
    sums = added(parts)
    slot = lax.broadcasted_iota(jnp.int32, (rowcap, rank), 0)
    empty = jnp.where(slot < count[0], 0.0, 1.0)
    out[...] = runs[...] * sums[:rowcap] / (sums[rowcap:] + empty)


def local(kernel, scalars, arrays, shapes, space=pltpu.VMEM, **more):
    near = pl.BlockSpec(memory_space=pltpu.VMEM)
    if space is pltpu.VMEM:
        arrays = [pltpu.with_memory_space_constraint(array, space) for array in arrays]
    return pl.pallas_call(
        kernel,
        out_shape=tuple(
            shape if hasattr(shape, "dtype") else pltpu.VMEM(shape, F32) for shape in shapes
        ),
        in_specs=[pl.BlockSpec(memory_space=pltpu.SMEM)] * len(scalars)
        + [pl.BlockSpec(memory_space=space)] * len(arrays),
        out_specs=(near,) * len(shapes),
        **more,
    )(*scalars, *arrays)


def shards(tensor, run_counts, run_init, bin_init, time_init):
    rowcap, rows, width = tensor.shape
    rank = run_init.shape[1]
    flat = tensor.reshape(rowcap * rows, width)
    plane = extent(PLANE)
    chunk = rank // plane
    index = lax.axis_index(PLANE).reshape(1)

    both, runs, run_gram, pick, flat, bins, _, times = local(
        terms_kernel,
        (run_counts, index),
        (flat, bin_init, run_init, time_init),
        (
            (extent(NEAR), 2 * rows, rank),
            (rowcap, rank),
            (rank, rank),
            (chunk, rank),
            pltpu.VMEM(flat.shape, flat.dtype),
            bin_init.shape,
            (rowcap, rank),
            (rows, rank),
        ),
        pl.ANY,
        scratch_shapes=[pltpu.SemaphoreType.DMA((4,))],
    )
    both = jnp.sum(exchange(both, NEAR), axis=0)
    both = exchange(jnp.broadcast_to(both[None], (extent(FAR),) + both.shape), FAR)
    both, times, time_gram = local(
        time_kernel,
        (),
        (both, times, runs, run_gram, flat),
        ((plane, chunk, width + rank), (rows, rank), (rank, rank)),
    )
    both = exchange(both, PLANE)
    (both,) = local(spread_kernel, (), (both,), ((extent(FAR), chunk, width + rank),))
    both = exchange(both, FAR)
    (mine,) = local(bins_kernel, (), (both, bins, pick), ((plane, chunk, width),))
    both, bins = local(
        runs_kernel,
        (),
        (exchange(mine, PLANE), flat, runs, times, time_gram),
        ((extent(TM), 2 * rowcap, rank), (rank, width)),
    )
    both = exchange(both, TM)
    result = jax.ShapeDtypeStruct((rowcap, rank), F32)
    (runs,) = local(last_kernel, (run_counts,), (both, runs), (result,))
    return (runs, bins.T, times)


def solution(mesh):
    fine = Mesh(mesh.devices.reshape(tuple(SIZES.values())), tuple(SIZES))
    return jax.shard_map(
        shards,
        mesh=fine,
        in_specs=(P(RUNS, TM, None), P(RUNS), P(RUNS, None), P(), P(TM, None)),
        out_specs=(P(RUNS, None), P(), P(TM, None)),
        check_vma=False,
    )
```

```python
import jax
import jax.numpy as jnp
from jax import lax
from jax.experimental import pallas as pl
from jax.experimental.pallas import tpu as pltpu
from jax.sharding import Mesh, PartitionSpec as P

HIGH = lax.Precision.HIGHEST
F32 = jnp.float32
BF16 = jnp.bfloat16
BLOCKS = 4
SIZES = {"x": 4, "h": 8, "l": 2, "y": 4, "c": 2}
RUNS = ("x", "h", "l")
NEAR = ("x", "l")
FAR = ("h",)
PLANE = ("x", "l", "y", "c")
TM = ("y", "c")
FIRST = (((0,), (0,)), ((), ()))
LAST = (((1,), (1,)), ((), ()))


def exact(left, right, dims):
    return lax.dot_general(left, right, dims, precision=HIGH, preferred_element_type=F32)


def quick(left, right, dims):
    return lax.dot_general(left, right, dims, preferred_element_type=F32)


def extent(axes):
    total = 1
    for axis in axes:
        total *= SIZES[axis]
    return total


def exchange(parts, axes):
    return lax.all_to_all(parts, axes, 0, 0)


def added(parts):
    total = parts[0]
    for part in range(1, parts.shape[0]):
        total += parts[part]
    return total


def terms_kernel(*refs):
    far, (both, runs_out, gram_out, pick, empty, *near), (number, sems) = refs[:5], refs[5:14], refs[14:]
    tensor, bins, run_init, times = near
    rowcap, rank = run_init.shape
    rows = times.shape[0]
    chunk = pick.shape[0]
    block = tensor.shape[0] // BLOCKS

    def part(i):
        return pl.ds(i * block, block)

    count_copy = pltpu.make_async_copy(far[4], number, sems.at[0])
    small = [pltpu.make_async_copy(far[i], near[i], sems.at[i]) for i in (2, 3)]
    bins_copy = pltpu.make_async_copy(far[1], bins, sems.at[1])
    large = [
        pltpu.make_async_copy(far[0].at[part(i)], tensor.at[part(i)], sems.at[4 + i])
        for i in range(BLOCKS)
    ]
    for copy in [count_copy, *small, bins_copy, *large]:
        copy.start()
    row = lax.broadcasted_iota(jnp.int32, (chunk, rank), 0) + lax.axis_index(PLANE) * chunk
    column = lax.broadcasted_iota(jnp.int32, (chunk, rank), 1)
    pick[...] = jnp.where(column == row, 1.0, 0.0)
    count_copy.wait()
    for copy in small:
        copy.wait()
    slot = lax.broadcasted_iota(jnp.int32, (rowcap, rank), 0)
    live = slot < number[0]
    empty[...] = jnp.where(live, 0.0, 1.0)
    runs = jnp.where(live, run_init[...], 0.0)
    runs_out[...] = runs
    run_gram = exact(runs, runs, FIRST)
    gram_out[...] = run_gram
    bins_copy.wait()
    full = bins[...]
    below = jnp.dot(times[...], run_gram * exact(full, full, FIRST), precision=HIGH)
    low = full.astype(BF16)
    for copy in range(both.shape[0]):
        both[copy, rows:] = below
    terms = None
    for i in range(BLOCKS):
        large[i].wait()
        inner = jnp.dot(tensor[part(i)], low, preferred_element_type=F32)
        for j in range(block // rows):
            slot = i * (block // rows) + j
            term = runs[slot : slot + 1] * inner[j * rows : (j + 1) * rows]
            terms = term if terms is None else terms + term
    for copy in range(both.shape[0]):
        both[copy, 0:rows] = terms


def time_kernel(parts, times, runs, run_gram, tensor, out, times_out, gram_out):
    rows, rank = times.shape
    rowcap = runs.shape[0]
    width = tensor.shape[1]
    sums = added(parts)
    new = times[...] * sums[:rows] / sums[rows:]
    times_out[...] = new
    time_gram = exact(new, new, FIRST)
    gram_out[...] = time_gram
    low = new.astype(BF16).astype(F32)
    left = jnp.concatenate([runs[i : i + 1] * low for i in range(rowcap)], axis=0)
    block = tensor[...]
    terms = None
    for _ in range(3):
        part = left.astype(BF16)
        term = quick(part, block, FIRST)
        terms = term if terms is None else terms + term
        left = left - part.astype(F32)
    out[:, :, 0:width] = terms.reshape(out.shape[0], out.shape[1], width)
    mixing = run_gram[...] * time_gram
    out[:, :, width:] = mixing.reshape(out.shape[0], out.shape[1], rank)


def spread_kernel(parts, out):
    total = added(parts)
    for copy in range(out.shape[0]):
        out[copy] = total


def bins_kernel(parts, bins, pick, out):
    count, chunk, width = out.shape
    sums = added(parts)
    left = jnp.concatenate([sums[:, width:], pick[...]], axis=0)
    got = exact(left, bins[...], LAST)
    mine = got[chunk:] * sums[:, :width] / got[:chunk]
    for copy in range(count):
        out[copy] = mine


def runs_kernel(parts, tensor, runs, times, time_gram, both, bins_out):
    rank, width = bins_out.shape
    rowcap = runs.shape[0]
    rows = times.shape[0]
    bins = parts[...].reshape(rank, width)
    bins_out[...] = bins
    inner = quick(tensor[...], bins.astype(BF16), LAST)
    mixing = exact(bins, bins, LAST) * time_gram[...]
    below = jnp.dot(runs[...], mixing, precision=HIGH)
    for copy in range(both.shape[0]):
        both[copy, rowcap:] = below
    for i in range(rowcap):
        term = jnp.sum(times[...] * inner[i * rows : (i + 1) * rows], axis=0, keepdims=True)
        for copy in range(both.shape[0]):
            both[copy, i : i + 1] = term


def last_kernel(parts, runs, empty, out):
    rowcap = runs.shape[0]
    sums = added(parts)
    out[...] = runs[...] * sums[:rowcap] / (sums[rowcap:] + empty[...])


def local(kernel, arrays, shapes, space=pltpu.VMEM, **more):
    if space is pltpu.VMEM:
        arrays = [pltpu.with_memory_space_constraint(array, space) for array in arrays]
    return pl.pallas_call(
        kernel,
        out_shape=tuple(
            shape if hasattr(shape, "dtype") else pltpu.VMEM(shape, F32) for shape in shapes
        ),
        in_specs=[pl.BlockSpec(memory_space=space)] * len(arrays),
        out_specs=(pl.BlockSpec(memory_space=pltpu.VMEM),) * len(shapes),
        **more,
    )(*arrays)


def shards(tensor, run_counts, run_init, bin_init, time_init):
    rowcap, rows, width = tensor.shape
    rank = run_init.shape[1]
    flat = tensor.reshape(rowcap * rows, width)
    plane = extent(PLANE)
    chunk = rank // plane

    both, runs, run_gram, pick, empty, flat, bins, _, times = local(
        terms_kernel,
        (flat, bin_init, run_init, time_init, run_counts),
        (
            (extent(NEAR), 2 * rows, rank),
            (rowcap, rank),
            (rank, rank),
            (chunk, rank),
            (rowcap, rank),
            pltpu.VMEM(flat.shape, flat.dtype),
            bin_init.shape,
            (rowcap, rank),
            (rows, rank),
        ),
        pl.ANY,
        scratch_shapes=[pltpu.SMEM((1,), jnp.int32), pltpu.SemaphoreType.DMA((4 + BLOCKS,))],
    )
    both = jnp.sum(exchange(both, NEAR), axis=0)
    both = exchange(jnp.broadcast_to(both[None], (extent(FAR),) + both.shape), FAR)
    both, times, time_gram = local(
        time_kernel,
        (both, times, runs, run_gram, flat),
        ((plane, chunk, width + rank), (rows, rank), (rank, rank)),
    )
    both = exchange(both, PLANE)
    (both,) = local(spread_kernel, (both,), ((extent(FAR), chunk, width + rank),))
    both = exchange(both, FAR)
    (mine,) = local(bins_kernel, (both, bins, pick), ((plane, chunk, width),))
    both, bins = local(
        runs_kernel,
        (exchange(mine, PLANE), flat, runs, times, time_gram),
        ((extent(TM), 2 * rowcap, rank), (rank, width)),
    )
    both = exchange(both, TM)
    result = jax.ShapeDtypeStruct((rowcap, rank), F32)
    (runs,) = local(last_kernel, (both, runs, empty), (result,))
    return (runs, bins.T, times)


def solution(mesh):
    fine = Mesh(mesh.devices.reshape(tuple(SIZES.values())), tuple(SIZES))
    return jax.shard_map(
        shards,
        mesh=fine,
        in_specs=(P(RUNS, TM, None), P(RUNS), P(RUNS, None), P(), P(TM, None)),
        out_specs=(P(RUNS, None), P(), P(TM, None)),
        check_vma=False,
    )
```

```python
import jax
import jax.numpy as jnp
from jax import lax
from jax.experimental import pallas as pl
from jax.experimental.pallas import tpu as pltpu
from jax.sharding import Mesh, PartitionSpec as P

HIGH = lax.Precision.HIGHEST
F32 = jnp.float32
BF16 = jnp.bfloat16
SIZES = {"x": 4, "h": 8, "l": 2, "y": 4, "c": 2}
RUNS = ("x", "h", "l")
NEAR = ("x", "l")
FAR = ("h",)
PLANE = ("x", "l", "y")
PAIR = ("c",)
TM = ("y", "c")
FIRST = (((0,), (0,)), ((), ()))
LAST = (((1,), (1,)), ((), ()))


def exact(left, right, dims):
    return lax.dot_general(left, right, dims, precision=HIGH, preferred_element_type=F32)


def quick(left, right, dims):
    return lax.dot_general(left, right, dims, preferred_element_type=F32)


def extent(axes):
    total = 1
    for axis in axes:
        total *= SIZES[axis]
    return total


def exchange(parts, axes):
    return lax.all_to_all(parts, axes, 0, 0)


def swap(value):
    return lax.ppermute(value, PAIR, [(0, 1), (1, 0)])


def added(parts):
    total = parts[0]
    for part in range(1, parts.shape[0]):
        total += parts[part]
    return total


def terms_kernel(count, index, *refs):
    far, (both, runs_out, gram_out, pick, *near), sems = refs[:4], refs[4:12], refs[12]
    tensor, bins, run_init, times = near
    copies = [pltpu.make_async_copy(far[i], near[i], sems.at[i]) for i in range(4)]
    for copy in reversed(copies):
        copy.start()
    rowcap, rank = run_init.shape
    rows = times.shape[0]
    chunk = pick.shape[0]
    row = lax.broadcasted_iota(jnp.int32, (chunk, rank), 0) + index[0]
    column = lax.broadcasted_iota(jnp.int32, (chunk, rank), 1)
    pick[...] = jnp.where(column == row, 1.0, 0.0)
    slot = lax.broadcasted_iota(jnp.int32, (rowcap, rank), 0)
    copies[2].wait()
    copies[3].wait()
    runs = jnp.where(slot < count[0], run_init[...], 0.0)
    runs_out[...] = runs
    run_gram = exact(runs, runs, FIRST)
    gram_out[...] = run_gram
    copies[1].wait()
    full = bins[...]
    below = jnp.dot(times[...], run_gram * exact(full, full, FIRST), precision=HIGH)
    copies[0].wait()
    inner = jnp.dot(tensor[...], full.astype(BF16), preferred_element_type=F32)
    terms = runs[0:1] * inner[0:rows]
    for i in range(1, rowcap):
        terms += runs[i : i + 1] * inner[i * rows : (i + 1) * rows]
    for copy in range(both.shape[0]):
        both[copy, 0:rows] = terms
        both[copy, rows:] = below


def time_kernel(parts, times, runs, run_gram, tensor, own, other, times_out, gram_out, whole):
    rows, rank = times.shape
    rowcap = runs.shape[0]
    width = tensor.shape[1]
    sums = added(parts)
    new = times[...] * sums[:rows] / sums[rows:]
    times_out[...] = new
    time_gram = exact(new, new, FIRST)
    gram_out[...] = time_gram
    low = new.astype(BF16).astype(F32)
    left = jnp.concatenate([runs[i : i + 1] * low for i in range(rowcap)], axis=0)
    block = tensor[...]
    terms = None
    for _ in range(3):
        part = left.astype(BF16)
        term = quick(part, block, FIRST)
        terms = term if terms is None else terms + term
        left = left - part.astype(F32)
    whole[:, 0:width] = terms
    whole[:, width:] = run_gram[...] * time_gram
    half = own.shape[0]
    core = lax.axis_index(PAIR)
    own[...] = whole[pl.ds(core * half, half)]
    other[...] = whole[pl.ds((1 - core) * half, half)]


def pair_kernel(own, other, out):
    out[...] = (own[...] + other[...]).reshape(out.shape)


def spread_kernel(parts, out):
    total = added(parts)
    for copy in range(out.shape[0]):
        out[copy] = total


def bins_kernel(parts, bins, pick, out):
    count, chunk, width = out.shape
    sums = added(parts)
    left = jnp.concatenate([sums[:, width:], pick[...]], axis=0)
    got = exact(left, bins[...], LAST)
    mine = got[chunk:] * sums[:, :width] / got[:chunk]
    for copy in range(count):
        out[copy] = mine


def half_kernel(parts, tensor, times, bins_out, terms_out):
    half, width = bins_out.shape
    rows = times.shape[0]
    core = lax.axis_index(PAIR)
    bins = parts[...].reshape(half, width)
    bins_out[...] = bins
    inner = quick(tensor[...], bins.astype(BF16), LAST)
    both = times[...]
    mine = jnp.where(core == 0, both[:, :half], both[:, half:])
    for i in range(terms_out.shape[0]):
        term = mine * inner[i * rows : (i + 1) * rows]
        terms_out[i : i + 1] = jnp.sum(term, axis=0, keepdims=True)


def runs_kernel(mine, own, parts, tensor, runs, times, time_gram, both, bins_out):
    half, width = own.shape
    rowcap = runs.shape[0]
    rows = times.shape[0]
    core = lax.axis_index(PAIR)
    rest = parts[...].reshape(half, width)
    bins_out[pl.ds(core * half, half)] = own[...]
    bins_out[pl.ds((1 - core) * half, half)] = rest
    bins = bins_out[...]
    inner = quick(tensor[...], rest.astype(BF16), LAST)
    mixing = exact(bins, bins, LAST) * time_gram[...]
    below = jnp.dot(runs[...], mixing, precision=HIGH)
    full = times[...]
    side = jnp.where(core == 0, full[:, half:], full[:, :half])
    found = [
        jnp.sum(side * inner[i * rows : (i + 1) * rows], axis=0, keepdims=True)
        for i in range(rowcap)
    ]
    found = jnp.concatenate(found, axis=0)
    first = jnp.where(core == 0, mine[...], found)
    second = jnp.where(core == 0, found, mine[...])
    terms = jnp.concatenate([first, second], axis=1)
    for copy in range(both.shape[0]):
        both[copy, rowcap:] = below
        both[copy, 0:rowcap] = terms


def last_kernel(count, parts, runs, out):
    rowcap, rank = runs.shape
    sums = added(parts)
    slot = lax.broadcasted_iota(jnp.int32, (rowcap, rank), 0)
    empty = jnp.where(slot < count[0], 0.0, 1.0)
    out[...] = runs[...] * sums[:rowcap] / (sums[rowcap:] + empty)


def local(kernel, scalars, arrays, shapes, space=pltpu.VMEM, **more):
    near = pl.BlockSpec(memory_space=pltpu.VMEM)
    if space is pltpu.VMEM:
        arrays = [pltpu.with_memory_space_constraint(array, space) for array in arrays]
    return pl.pallas_call(
        kernel,
        out_shape=tuple(
            shape if hasattr(shape, "dtype") else pltpu.VMEM(shape, F32) for shape in shapes
        ),
        in_specs=[pl.BlockSpec(memory_space=pltpu.SMEM)] * len(scalars)
        + [pl.BlockSpec(memory_space=space)] * len(arrays),
        out_specs=(near,) * len(shapes),
        **more,
    )(*scalars, *arrays)


def shards(tensor, run_counts, run_init, bin_init, time_init):
    rowcap, rows, width = tensor.shape
    rank = run_init.shape[1]
    flat = tensor.reshape(rowcap * rows, width)
    plane = extent(PLANE)
    chunk = rank // (plane * extent(PAIR))
    half = rank // extent(PAIR)
    index = (lax.axis_index(PAIR) * half + lax.axis_index(PLANE) * chunk).reshape(1)

    both, runs, run_gram, pick, flat, bins, _, times = local(
        terms_kernel,
        (run_counts, index),
        (flat, bin_init, run_init, time_init),
        (
            (extent(NEAR), 2 * rows, rank),
            (rowcap, rank),
            (rank, rank),
            (chunk, rank),
            pltpu.VMEM(flat.shape, flat.dtype),
            bin_init.shape,
            (rowcap, rank),
            (rows, rank),
        ),
        pl.ANY,
        scratch_shapes=[pltpu.SemaphoreType.DMA((4,))],
    )
    both = jnp.sum(exchange(both, NEAR), axis=0)
    both = exchange(jnp.broadcast_to(both[None], (extent(FAR),) + both.shape), FAR)
    own, other, times, time_gram = local(
        time_kernel,
        (),
        (both, times, runs, run_gram, flat),
        ((half, width + rank), (half, width + rank), (rows, rank), (rank, rank)),
        scratch_shapes=[pltpu.VMEM((rank, width + rank), F32)],
    )
    other = swap(other)
    (both,) = local(pair_kernel, (), (own, other), ((plane, chunk, width + rank),))
    both = exchange(both, PLANE)
    (both,) = local(spread_kernel, (), (both,), ((extent(FAR), chunk, width + rank),))
    both = exchange(both, FAR)
    (mine,) = local(bins_kernel, (), (both, bins, pick), ((plane, chunk, width),))
    mine = exchange(mine, PLANE)
    rest = swap(mine)
    own, terms = local(half_kernel, (), (mine, flat, times), ((half, width), (rowcap, half)))
    both, bins = local(
        runs_kernel,
        (),
        (terms, own, rest, flat, runs, times, time_gram),
        ((extent(TM), 2 * rowcap, rank), (rank, width)),
    )
    both = exchange(both, TM)
    result = jax.ShapeDtypeStruct((rowcap, rank), F32)
    (runs,) = local(last_kernel, (run_counts,), (both, runs), (result,))
    return (runs, bins.T, times)


def solution(mesh):
    fine = Mesh(mesh.devices.reshape(tuple(SIZES.values())), tuple(SIZES))
    return jax.shard_map(
        shards,
        mesh=fine,
        in_specs=(P(RUNS, TM, None), P(RUNS), P(RUNS, None), P(), P(TM, None)),
        out_specs=(P(RUNS, None), P(), P(TM, None)),
        check_vma=False,
    )
```

```python
import jax
import jax.numpy as jnp
from jax import lax
from jax.experimental import pallas as pl
from jax.experimental.pallas import tpu as pltpu
from jax.sharding import Mesh, PartitionSpec as P

HIGH = lax.Precision.HIGHEST
F32 = jnp.float32
BF16 = jnp.bfloat16
SIZES = {"x": 4, "h": 8, "l": 2, "y": 4, "c": 2}
RUNS = ("x", "h", "l")
NEAR = ("x", "l")
FAR = ("h",)
PLANE = ("x", "l", "y")
PAIR = ("c",)
TM = ("y", "c")
FIRST = (((0,), (0,)), ((), ()))
LAST = (((1,), (1,)), ((), ()))


def exact(left, right, dims):
    return lax.dot_general(left, right, dims, precision=HIGH, preferred_element_type=F32)


def quick(left, right, dims):
    return lax.dot_general(left, right, dims, preferred_element_type=F32)


def extent(axes):
    total = 1
    for axis in axes:
        total *= SIZES[axis]
    return total


def exchange(parts, axes):
    return lax.all_to_all(parts, axes, 0, 0)


def swap(value):
    return lax.ppermute(value, PAIR, [(0, 1), (1, 0)])


def added(parts):
    total = parts[0]
    for part in range(1, parts.shape[0]):
        total += parts[part]
    return total


def terms_kernel(*refs):
    far, (both, runs_out, gram_out, empty, *near), (sems,) = refs[:5], refs[5:13], refs[13:]
    tensor, bins, run_init, times = near
    copies = [pltpu.make_async_copy(far[i], near[i], sems.at[i]) for i in range(4)]
    for copy in reversed(copies):
        copy.start()
    rowcap, rank = run_init.shape
    rows = times.shape[0]
    slot = lax.broadcasted_iota(jnp.int32, (rowcap, rank), 0)
    for copy in reversed(copies[2:]):
        copy.wait()
    live = slot < far[4][0]
    empty[...] = jnp.where(live, 0.0, 1.0)
    runs = jnp.where(live, run_init[...], 0.0)
    runs_out[...] = runs
    run_gram = exact(runs, runs, FIRST)
    gram_out[...] = run_gram
    copies[1].wait()
    full = bins[...]
    below = jnp.dot(times[...], run_gram * exact(full, full, FIRST), precision=HIGH)
    copies[0].wait()
    inner = jnp.dot(tensor[...], full.astype(BF16), preferred_element_type=F32)
    terms = runs[0:1] * inner[0:rows]
    for i in range(1, rowcap):
        terms += runs[i : i + 1] * inner[i * rows : (i + 1) * rows]
    for copy in range(both.shape[0]):
        both[copy, 0:rows] = terms
        both[copy, rows:] = below


def pieces(value):
    out = []
    for _ in range(3):
        out.append(value.astype(BF16))
        value = value - out[-1].astype(F32)
    return out


def half_terms(runs, times, tensor, side):
    half = runs.shape[1] // 2
    runs, times = runs[...], times[...]
    low = times.astype(BF16).astype(F32)
    runs = jnp.where(side == 0, runs[:, :half], runs[:, half:])
    low = jnp.where(side == 0, low[:, :half], low[:, half:])
    left = jnp.concatenate([runs[i : i + 1] * low for i in range(runs.shape[0])], axis=0)
    block = tensor[...]
    high, mid, rest = (quick(part, block, FIRST) for part in pieces(left))
    return high + mid + rest


def time_kernel(parts, times, runs, run_gram, tensor, other, mixed, times_out, gram_out, whole):
    rows = times.shape[0]
    width = tensor.shape[1]
    half = other.shape[0]
    core = lax.axis_index(PAIR)
    sums = added(parts)
    new = times[...] * sums[:rows] / sums[rows:]
    times_out[...] = new
    time_gram = exact(new, new, FIRST)
    gram_out[...] = time_gram
    whole[...] = run_gram[...] * time_gram
    mixed[...] = whole[pl.ds(core * half, half)]
    other[:, 0:width] = half_terms(runs, times_out, tensor, 1 - core)
    other[:, width:] = whole[pl.ds((1 - core) * half, half)]


def side_kernel(runs, times, tensor, bins, own, *parts):
    own[...] = half_terms(runs, times, tensor, lax.axis_index(PAIR))
    for ref, part in zip(parts, pieces(bins[...].T)):
        ref[...] = part


def pair_kernel(own, mixed, other, out):
    count, chunk, width = out.shape
    inner = own.shape[1]
    got = other[...]
    out[:, :, 0:inner] = (own[...] + got[:, :inner]).reshape(count, chunk, inner)
    out[:, :, inner:] = (mixed[...] + got[:, inner:]).reshape(count, chunk, width - inner)


def spread_kernel(parts, out):
    total = added(parts)
    for copy in range(out.shape[0]):
        out[copy] = total


def bins_kernel(parts, high, mid, low, out):
    count, chunk, width = out.shape
    rank = high.shape[0]
    start = lax.axis_index(PAIR) * (count * chunk) + lax.axis_index(PLANE) * chunk
    sums = added(parts)
    row = lax.broadcasted_iota(jnp.int32, (chunk, rank), 0) + start
    column = lax.broadcasted_iota(jnp.int32, (chunk, rank), 1)
    pick = jnp.where(column == row, 1.0, 0.0)
    split = [part.astype(F32) for part in pieces(sums[:, width:])]
    left = jnp.concatenate([*split, pick], axis=0).astype(BF16)
    first, second, third = (jnp.dot(left, ref[...], preferred_element_type=F32) for ref in (high, mid, low))
    a, b, c, d = (slice(i * chunk, (i + 1) * chunk) for i in range(4))
    below = first[a] + (first[b] + second[a]) + (first[c] + second[b] + third[a])
    mine = (first[d] + second[d] + third[d]) * sums[:, :width] / below
    for copy in range(count):
        out[copy] = mine


def half_kernel(parts, tensor, times, bins_out, terms_out):
    half, width = bins_out.shape
    rows = times.shape[0]
    core = lax.axis_index(PAIR)
    bins = parts[...].reshape(half, width)
    bins_out[...] = bins
    inner = quick(tensor[...], bins.astype(BF16), LAST)
    both = times[...]
    mine = jnp.where(core == 0, both[:, :half], both[:, half:])
    for i in range(terms_out.shape[0]):
        term = mine * inner[i * rows : (i + 1) * rows]
        terms_out[i : i + 1] = jnp.sum(term, axis=0, keepdims=True)


def runs_kernel(mine, own, parts, tensor, runs, times, time_gram, both, bins_out):
    half, width = own.shape
    rowcap = runs.shape[0]
    rows = times.shape[0]
    core = lax.axis_index(PAIR)
    rest = parts[...].reshape(half, width)
    bins_out[pl.ds(core * half, half)] = own[...]
    bins_out[pl.ds((1 - core) * half, half)] = rest
    bins = bins_out[...]
    inner = quick(tensor[...], rest.astype(BF16), LAST)
    mixing = exact(bins, bins, LAST) * time_gram[...]
    below = jnp.dot(runs[...], mixing, precision=HIGH)
    full = times[...]
    side = jnp.where(core == 0, full[:, half:], full[:, :half])
    found = [
        jnp.sum(side * inner[i * rows : (i + 1) * rows], axis=0, keepdims=True)
        for i in range(rowcap)
    ]
    found = jnp.concatenate(found, axis=0)
    first = jnp.where(core == 0, mine[...], found)
    second = jnp.where(core == 0, found, mine[...])
    terms = jnp.concatenate([first, second], axis=1)
    for copy in range(both.shape[0]):
        both[copy, rowcap:] = below
        both[copy, 0:rowcap] = terms


def last_kernel(parts, runs, empty, out):
    rowcap = runs.shape[0]
    sums = added(parts)
    out[...] = runs[...] * sums[:rowcap] / (sums[rowcap:] + empty[...])


def shape_of(shape, dtype=F32):
    return pltpu.VMEM(shape, dtype)


def local(kernel, arrays, shapes, specs=None, **more):
    near = pl.BlockSpec(memory_space=pltpu.VMEM)
    if specs is None:
        arrays = [pltpu.with_memory_space_constraint(array, pltpu.VMEM) for array in arrays]
    return pl.pallas_call(
        kernel,
        out_shape=tuple(shapes),
        in_specs=specs or [near] * len(arrays),
        out_specs=(near,) * len(shapes),
        **more,
    )(*arrays)


def shards(tensor, run_counts, run_init, bin_init, time_init):
    rowcap, rows, width = tensor.shape
    rank = run_init.shape[1]
    flat = tensor.reshape(rowcap * rows, width)
    plane = extent(PLANE)
    half = rank // extent(PAIR)
    chunk = half // plane
    wide = width + rank

    both, runs, run_gram, empty, flat, bins, _, times = local(
        terms_kernel,
        (flat, bin_init, run_init, time_init, run_counts),
        (
            shape_of((extent(NEAR), 2 * rows, rank)),
            shape_of((rowcap, rank)),
            shape_of((rank, rank)),
            shape_of((rowcap, rank)),
            shape_of(flat.shape, flat.dtype),
            shape_of(bin_init.shape),
            shape_of((rowcap, rank)),
            shape_of((rows, rank)),
        ),
        [pl.BlockSpec(memory_space=pl.ANY)] * 4 + [pl.BlockSpec(memory_space=pltpu.SMEM)],
        scratch_shapes=[pltpu.SemaphoreType.DMA((4,))],
    )
    both = jnp.sum(exchange(both, NEAR), axis=0)
    both = exchange(jnp.broadcast_to(both[None], (extent(FAR),) + both.shape), FAR)
    other, mixed, times, time_gram = local(
        time_kernel,
        (both, times, runs, run_gram, flat),
        (shape_of((half, wide)), shape_of((half, rank)), shape_of((rows, rank)), shape_of((rank, rank))),
        scratch_shapes=[pltpu.VMEM((rank, rank), F32)],
    )
    other = swap(other)
    own, *parts = local(
        side_kernel,
        (runs, times, flat, bins),
        [shape_of((half, width))] + [shape_of((rank, width), BF16)] * 3,
    )
    (both,) = local(pair_kernel, (own, mixed, other), [shape_of((plane, chunk, wide))])
    both = exchange(both, PLANE)
    (both,) = local(spread_kernel, (both,), [shape_of((extent(FAR), chunk, wide))])
    both = exchange(both, FAR)
    (mine,) = local(bins_kernel, (both, *parts), [shape_of((plane, chunk, width))])
    mine = exchange(mine, PLANE)
    rest = swap(mine)
    own, terms = local(
        half_kernel, (mine, flat, times), (shape_of((half, width)), shape_of((rowcap, half)))
    )
    both, bins = local(
        runs_kernel,
        (terms, own, rest, flat, runs, times, time_gram),
        (shape_of((extent(TM), 2 * rowcap, rank)), shape_of((rank, width))),
    )
    both = exchange(both, TM)
    result = jax.ShapeDtypeStruct((rowcap, rank), F32)
    (runs,) = local(last_kernel, (both, runs, empty), [result])
    return (runs, bins.T, times)


def solution(mesh):
    fine = Mesh(mesh.devices.reshape(tuple(SIZES.values())), tuple(SIZES))
    return jax.shard_map(
        shards,
        mesh=fine,
        in_specs=(P(RUNS, TM, None), P(RUNS), P(RUNS, None), P(), P(TM, None)),
        out_specs=(P(RUNS, None), P(), P(TM, None)),
        check_vma=False,
    )
```

```python
import jax
import jax.numpy as jnp
from jax import lax
from jax.experimental import pallas as pl
from jax.experimental.pallas import tpu as pltpu
from jax.sharding import Mesh, PartitionSpec as P

HIGH = lax.Precision.HIGHEST
F32 = jnp.float32
BF16 = jnp.bfloat16
SIZES = {"x": 4, "h": 8, "l": 2, "y": 4, "c": 2}
RUNS = ("x", "h", "l")
NEAR = ("x", "l")
FAR = ("h",)
PLANE = ("x", "l", "y")
PAIR = ("c",)
TM = ("y", "c")
FIRST = (((0,), (0,)), ((), ()))
LAST = (((1,), (1,)), ((), ()))


def exact(left, right, dims):
    return lax.dot_general(left, right, dims, precision=HIGH, preferred_element_type=F32)


def quick(left, right, dims):
    return lax.dot_general(left, right, dims, preferred_element_type=F32)


def extent(axes):
    total = 1
    for axis in axes:
        total *= SIZES[axis]
    return total


def exchange(parts, axes):
    return lax.all_to_all(parts, axes, 0, 0)


def swap(value):
    return lax.ppermute(value, PAIR, [(0, 1), (1, 0)])


def added(parts):
    total = parts[0]
    for part in range(1, parts.shape[0]):
        total += parts[part]
    return total


def terms_kernel(*refs):
    far, (both, runs_out, gram_out, empty, *near), (sems,) = refs[:5], refs[5:13], refs[13:]
    tensor, bins, run_init, times = near
    copies = [pltpu.make_async_copy(far[i], near[i], sems.at[i]) for i in range(4)]
    for copy in reversed(copies):
        copy.start()
    rowcap, rank = run_init.shape
    rows = times.shape[0]
    slot = lax.broadcasted_iota(jnp.int32, (rowcap, rank), 0)
    for copy in reversed(copies[2:]):
        copy.wait()
    live = slot < far[4][0]
    empty[...] = jnp.where(live, 0.0, 1.0)
    runs = jnp.where(live, run_init[...], 0.0)
    runs_out[...] = runs
    run_gram = exact(runs, runs, FIRST)
    gram_out[...] = run_gram
    copies[1].wait()
    full = bins[...]
    below = jnp.dot(times[...], run_gram * exact(full, full, FIRST), precision=HIGH)
    copies[0].wait()
    inner = jnp.dot(tensor[...], full.astype(BF16), preferred_element_type=F32)
    terms = runs[0:1] * inner[0:rows]
    for i in range(1, rowcap):
        terms += runs[i : i + 1] * inner[i * rows : (i + 1) * rows]
    for copy in range(both.shape[0]):
        both[copy, 0:rows] = terms
        both[copy, rows:] = below


def pieces(value):
    out = []
    for _ in range(3):
        out.append(value.astype(BF16))
        value = value - out[-1].astype(F32)
    return out


def half_terms(runs, times, tensor, side):
    half = runs.shape[1] // 2
    runs, times = runs[...], times[...]
    low = times.astype(BF16).astype(F32)
    runs = jnp.where(side == 0, runs[:, :half], runs[:, half:])
    low = jnp.where(side == 0, low[:, :half], low[:, half:])
    left = jnp.concatenate([runs[i : i + 1] * low for i in range(runs.shape[0])], axis=0)
    block = tensor[...]
    high, mid, rest = (quick(part, block, FIRST) for part in pieces(left))
    return high + mid + rest


def time_kernel(parts, times, runs, run_gram, tensor, other, mixed, times_out, gram_out, whole):
    rows = times.shape[0]
    width = tensor.shape[1]
    half = other.shape[0]
    core = lax.axis_index(PAIR)
    sums = added(parts)
    new = times[...] * sums[:rows] / sums[rows:]
    times_out[...] = new
    time_gram = exact(new, new, FIRST)
    gram_out[...] = time_gram
    whole[...] = run_gram[...] * time_gram
    mixed[...] = whole[pl.ds(core * half, half)]
    other[:, 0:width] = half_terms(runs, times_out, tensor, 1 - core)
    other[:, width:] = whole[pl.ds((1 - core) * half, half)]


def side_kernel(runs, times, tensor, bins, own, *parts):
    own[...] = half_terms(runs, times, tensor, lax.axis_index(PAIR))
    for ref, part in zip(parts, pieces(bins[...].T)):
        ref[...] = part


def pair_kernel(own, mixed, other, out):
    count, chunk, width = out.shape
    inner = own.shape[1]
    got = other[...]
    out[:, :, 0:inner] = (own[...] + got[:, :inner]).reshape(count, chunk, inner)
    out[:, :, inner:] = (mixed[...] + got[:, inner:]).reshape(count, chunk, width - inner)


def spread_kernel(parts, out):
    total = added(parts)
    for copy in range(out.shape[0]):
        out[copy] = total


def bins_kernel(parts, high, mid, low, out):
    count, chunk, width = out.shape
    rank = high.shape[0]
    start = lax.axis_index(PAIR) * (count * chunk) + lax.axis_index(PLANE) * chunk
    sums = added(parts)
    row = lax.broadcasted_iota(jnp.int32, (chunk, rank), 0) + start
    column = lax.broadcasted_iota(jnp.int32, (chunk, rank), 1)
    pick = jnp.where(column == row, 1.0, 0.0)
    split = [part.astype(F32) for part in pieces(sums[:, width:])]
    left = jnp.concatenate([*split, pick], axis=0).astype(BF16)
    first, second, third = (jnp.dot(left, ref[...], preferred_element_type=F32) for ref in (high, mid, low))
    a, b, c, d = (slice(i * chunk, (i + 1) * chunk) for i in range(4))
    below = first[a] + (first[b] + second[a]) + (first[c] + second[b] + third[a])
    mine = (first[d] + second[d] + third[d]) * sums[:, :width] / below
    for copy in range(count):
        out[copy] = mine


def half_kernel(parts, tensor, times, bins_out, terms_out):
    half, width = bins_out.shape
    rows = times.shape[0]
    core = lax.axis_index(PAIR)
    bins = parts[...].reshape(half, width)
    bins_out[...] = bins
    inner = quick(tensor[...], bins.astype(BF16), LAST)
    both = times[...]
    mine = jnp.where(core == 0, both[:, :half], both[:, half:])
    for i in range(terms_out.shape[0]):
        term = mine * inner[i * rows : (i + 1) * rows]
        terms_out[i : i + 1] = jnp.sum(term, axis=0, keepdims=True)


def runs_kernel(mine, own, parts, tensor, runs, times, time_gram, both, turned, bins_out):
    half, width = own.shape
    rowcap = runs.shape[0]
    rows = times.shape[0]
    core = lax.axis_index(PAIR)
    rest = parts[...].reshape(half, width)
    bins_out[pl.ds(core * half, half)] = own[...]
    bins_out[pl.ds((1 - core) * half, half)] = rest
    bins = bins_out[...]
    turned[...] = bins.T
    inner = quick(tensor[...], rest.astype(BF16), LAST)
    mixing = exact(bins, bins, LAST) * time_gram[...]
    below = jnp.dot(runs[...], mixing, precision=HIGH)
    full = times[...]
    side = jnp.where(core == 0, full[:, half:], full[:, :half])
    found = [
        jnp.sum(side * inner[i * rows : (i + 1) * rows], axis=0, keepdims=True)
        for i in range(rowcap)
    ]
    found = jnp.concatenate(found, axis=0)
    first = jnp.where(core == 0, mine[...], found)
    second = jnp.where(core == 0, found, mine[...])
    terms = jnp.concatenate([first, second], axis=1)
    for copy in range(both.shape[0]):
        both[copy, rowcap:] = below
        both[copy, 0:rowcap] = terms


def last_kernel(parts, runs, empty, bins, times, runs_out, bins_out, times_out, new, sems):
    copies = [
        pltpu.make_async_copy(near, far, sems.at[i])
        for i, (near, far) in enumerate(((bins, bins_out), (times, times_out), (new, runs_out)))
    ]
    copies[0].start()
    copies[1].start()
    rowcap = runs.shape[0]
    sums = added(parts)
    new[...] = runs[...] * sums[:rowcap] / (sums[rowcap:] + empty[...])
    copies[2].start()
    for copy in copies:
        copy.wait()


def shape_of(shape, dtype=F32):
    return pltpu.VMEM(shape, dtype)


def local(kernel, arrays, shapes, specs=None, outs=pltpu.VMEM, **more):
    near = pl.BlockSpec(memory_space=pltpu.VMEM)
    if specs is None:
        arrays = [pltpu.with_memory_space_constraint(array, pltpu.VMEM) for array in arrays]
    return pl.pallas_call(
        kernel,
        out_shape=tuple(shapes),
        in_specs=specs or [near] * len(arrays),
        out_specs=(pl.BlockSpec(memory_space=outs),) * len(shapes),
        **more,
    )(*arrays)


def shards(tensor, run_counts, run_init, bin_init, time_init):
    rowcap, rows, width = tensor.shape
    rank = run_init.shape[1]
    flat = tensor.reshape(rowcap * rows, width)
    plane = extent(PLANE)
    half = rank // extent(PAIR)
    chunk = half // plane
    wide = width + rank

    both, runs, run_gram, empty, flat, bins, _, times = local(
        terms_kernel,
        (flat, bin_init, run_init, time_init, run_counts),
        (
            shape_of((extent(NEAR), 2 * rows, rank)),
            shape_of((rowcap, rank)),
            shape_of((rank, rank)),
            shape_of((rowcap, rank)),
            shape_of(flat.shape, flat.dtype),
            shape_of(bin_init.shape),
            shape_of((rowcap, rank)),
            shape_of((rows, rank)),
        ),
        [pl.BlockSpec(memory_space=pl.ANY)] * 4 + [pl.BlockSpec(memory_space=pltpu.SMEM)],
        scratch_shapes=[pltpu.SemaphoreType.DMA((4,))],
    )
    both = jnp.sum(exchange(both, NEAR), axis=0)
    both = exchange(jnp.broadcast_to(both[None], (extent(FAR),) + both.shape), FAR)
    other, mixed, times, time_gram = local(
        time_kernel,
        (both, times, runs, run_gram, flat),
        (shape_of((half, wide)), shape_of((half, rank)), shape_of((rows, rank)), shape_of((rank, rank))),
        scratch_shapes=[pltpu.VMEM((rank, rank), F32)],
    )
    other = swap(other)
    own, *parts = local(
        side_kernel,
        (runs, times, flat, bins),
        [shape_of((half, width))] + [shape_of((rank, width), BF16)] * 3,
    )
    (both,) = local(pair_kernel, (own, mixed, other), [shape_of((plane, chunk, wide))])
    both = exchange(both, PLANE)
    (both,) = local(spread_kernel, (both,), [shape_of((extent(FAR), chunk, wide))])
    both = exchange(both, FAR)
    (mine,) = local(bins_kernel, (both, *parts), [shape_of((plane, chunk, width))])
    mine = exchange(mine, PLANE)
    rest = swap(mine)
    own, terms = local(
        half_kernel, (mine, flat, times), (shape_of((half, width)), shape_of((rowcap, half)))
    )
    both, bins = local(
        runs_kernel,
        (terms, own, rest, flat, runs, times, time_gram),
        (shape_of((extent(TM), 2 * rowcap, rank)), shape_of((width, rank))),
        scratch_shapes=[pltpu.VMEM((rank, width), F32)],
    )
    return tuple(
        local(
            last_kernel,
            (exchange(both, TM), runs, empty, bins, times),
            [jax.ShapeDtypeStruct(shape, F32) for shape in (runs.shape, bins.shape, times.shape)],
            outs=pl.ANY,
            scratch_shapes=[pltpu.VMEM(runs.shape, F32), pltpu.SemaphoreType.DMA((3,))],
        )
    )


def solution(mesh):
    fine = Mesh(mesh.devices.reshape(tuple(SIZES.values())), tuple(SIZES))
    return jax.shard_map(
        shards,
        mesh=fine,
        in_specs=(P(RUNS, TM, None), P(RUNS), P(RUNS, None), P(), P(TM, None)),
        out_specs=(P(RUNS, None), P(), P(TM, None)),
        check_vma=False,
    )
```

```python
import jax
import jax.numpy as jnp
from jax import lax
from jax.experimental import pallas as pl
from jax.experimental.pallas import tpu as pltpu
from jax.sharding import Mesh, PartitionSpec as P

HIGH = lax.Precision.HIGHEST
F32 = jnp.float32
BF16 = jnp.bfloat16
SIZES = {"x": 4, "h": 8, "l": 2, "y": 4, "c": 2}
RUNS = ("x", "h", "l")
NEAR = ("x", "l")
FAR = ("h",)
PLANE = ("x", "l", "y")
PAIR = ("c",)
TM = ("y", "c")
FIRST = (((0,), (0,)), ((), ()))
LAST = (((1,), (1,)), ((), ()))


def exact(left, right, dims):
    return lax.dot_general(left, right, dims, precision=HIGH, preferred_element_type=F32)


def quick(left, right, dims):
    return lax.dot_general(left, right, dims, preferred_element_type=F32)


def extent(axes):
    total = 1
    for axis in axes:
        total *= SIZES[axis]
    return total


def exchange(parts, axes):
    return lax.all_to_all(parts, axes, 0, 0)


def swap(value):
    return lax.ppermute(value, PAIR, [(0, 1), (1, 0)])


def added(parts):
    total = parts[0]
    for part in range(1, parts.shape[0]):
        total += parts[part]
    return total


def grams_kernel(*refs):
    far, count = refs[:3], refs[3]
    runs_out, gram_out, empty, low, below, *near, sems = refs[4:]
    bins, run_init, times = near
    copies = [pltpu.make_async_copy(far[i], near[i], sems.at[i]) for i in range(3)]
    for copy in reversed(copies):
        copy.start()
    slot = lax.broadcasted_iota(jnp.int32, run_init.shape, 0)
    copies[1].wait()
    live = slot < count[0]
    empty[...] = jnp.where(live, 0.0, 1.0)
    runs = jnp.where(live, run_init[...], 0.0)
    runs_out[...] = runs
    run_gram = exact(runs, runs, FIRST)
    gram_out[...] = run_gram
    copies[2].wait()
    copies[0].wait()
    full = bins[...]
    low[...] = full.astype(BF16)
    below[...] = jnp.dot(times[...], run_gram * square(full, FIRST), precision=HIGH)


def terms_kernel(tensor, low, runs, below, both):
    rowcap = runs.shape[0]
    rows = below.shape[0]
    inner = jnp.dot(tensor[...], low[...], preferred_element_type=F32)
    terms = runs[0:1] * inner[0:rows]
    for i in range(1, rowcap):
        terms += runs[i : i + 1] * inner[i * rows : (i + 1) * rows]
    for copy in range(both.shape[0]):
        both[copy, 0:rows] = terms
        both[copy, rows:] = below[...]


def pieces(value):
    out = []
    for _ in range(3):
        out.append(value.astype(BF16))
        value = value - out[-1].astype(F32)
    return out


def square(value, dims):
    high, mid, low = pieces(value)
    cross = quick(high, mid, dims)
    far = quick(high, low, dims)
    return quick(high, high, dims) + (cross + cross.T) + (quick(mid, mid, dims) + far + far.T)


def half_terms(runs, times, tensor, side):
    half = runs.shape[1] // 2
    runs, times = runs[...], times[...]
    low = times.astype(BF16).astype(F32)
    runs = jnp.where(side == 0, runs[:, :half], runs[:, half:])
    low = jnp.where(side == 0, low[:, :half], low[:, half:])
    left = jnp.concatenate([runs[i : i + 1] * low for i in range(runs.shape[0])], axis=0)
    block = tensor[...]
    high, mid, rest = (quick(part, block, FIRST) for part in pieces(left))
    return high + mid + rest


def time_kernel(parts, times, runs, run_gram, tensor, other, mixed, times_out, gram_out, whole):
    rows = times.shape[0]
    width = tensor.shape[1]
    half = other.shape[0]
    core = lax.axis_index(PAIR)
    sums = added(parts)
    new = times[...] * sums[:rows] / sums[rows:]
    times_out[...] = new
    time_gram = exact(new, new, FIRST)
    gram_out[...] = time_gram
    whole[...] = run_gram[...] * time_gram
    mixed[...] = whole[pl.ds(core * half, half)]
    other[:, 0:width] = half_terms(runs, times_out, tensor, 1 - core)
    other[:, width:] = whole[pl.ds((1 - core) * half, half)]


def side_kernel(runs, times, tensor, bins, own, *parts):
    own[...] = half_terms(runs, times, tensor, lax.axis_index(PAIR))
    for ref, part in zip(parts, pieces(bins[...].T)):
        ref[...] = part


def pair_kernel(own, mixed, other, out):
    count, chunk, width = out.shape
    inner = own.shape[1]
    got = other[...]
    out[:, :, 0:inner] = (own[...] + got[:, :inner]).reshape(count, chunk, inner)
    out[:, :, inner:] = (mixed[...] + got[:, inner:]).reshape(count, chunk, width - inner)


def spread_kernel(parts, out):
    total = added(parts)
    for copy in range(out.shape[0]):
        out[copy] = total


def bins_kernel(parts, high, mid, low, out):
    count, chunk, width = out.shape
    rank = high.shape[0]
    start = lax.axis_index(PAIR) * (count * chunk) + lax.axis_index(PLANE) * chunk
    sums = added(parts)
    row = lax.broadcasted_iota(jnp.int32, (chunk, rank), 0) + start
    column = lax.broadcasted_iota(jnp.int32, (chunk, rank), 1)
    pick = jnp.where(column == row, 1.0, 0.0)
    split = [part.astype(F32) for part in pieces(sums[:, width:])]
    left = jnp.concatenate([*split, pick], axis=0).astype(BF16)
    first, second, third = (jnp.dot(left, ref[...], preferred_element_type=F32) for ref in (high, mid, low))
    a, b, c, d = (slice(i * chunk, (i + 1) * chunk) for i in range(4))
    below = first[a] + (first[b] + second[a]) + (first[c] + second[b] + third[a])
    mine = (first[d] + second[d] + third[d]) * sums[:, :width] / below
    for copy in range(count):
        out[copy] = mine


def half_kernel(parts, tensor, times, bins_out, terms_out):
    half, width = bins_out.shape
    rows = times.shape[0]
    core = lax.axis_index(PAIR)
    bins = parts[...].reshape(half, width)
    bins_out[...] = bins
    inner = quick(tensor[...], bins.astype(BF16), LAST)
    both = times[...]
    mine = jnp.where(core == 0, both[:, :half], both[:, half:])
    for i in range(terms_out.shape[0]):
        term = mine * inner[i * rows : (i + 1) * rows]
        terms_out[i : i + 1] = jnp.sum(term, axis=0, keepdims=True)


def runs_kernel(mine, own, parts, tensor, runs, times, time_gram, both, turned, bins_out):
    half, width = own.shape
    rowcap = runs.shape[0]
    rows = times.shape[0]
    core = lax.axis_index(PAIR)
    rest = parts[...].reshape(half, width)
    bins_out[pl.ds(core * half, half)] = own[...]
    bins_out[pl.ds((1 - core) * half, half)] = rest
    bins = bins_out[...]
    turned[...] = bins.T
    inner = quick(tensor[...], rest.astype(BF16), LAST)
    mixing = exact(bins, bins, LAST) * time_gram[...]
    below = jnp.dot(runs[...], mixing, precision=HIGH)
    full = times[...]
    side = jnp.where(core == 0, full[:, half:], full[:, :half])
    found = [
        jnp.sum(side * inner[i * rows : (i + 1) * rows], axis=0, keepdims=True)
        for i in range(rowcap)
    ]
    found = jnp.concatenate(found, axis=0)
    first = jnp.where(core == 0, mine[...], found)
    second = jnp.where(core == 0, found, mine[...])
    terms = jnp.concatenate([first, second], axis=1)
    for copy in range(both.shape[0]):
        both[copy, rowcap:] = below
        both[copy, 0:rowcap] = terms


def last_kernel(parts, runs, empty, bins, times, runs_out, bins_out, times_out, new, sems):
    copies = [
        pltpu.make_async_copy(near, far, sems.at[i])
        for i, (near, far) in enumerate(((bins, bins_out), (times, times_out), (new, runs_out)))
    ]
    copies[0].start()
    copies[1].start()
    rowcap = runs.shape[0]
    sums = added(parts)
    new[...] = runs[...] * sums[:rowcap] / (sums[rowcap:] + empty[...])
    copies[2].start()
    for copy in copies:
        copy.wait()


def shape_of(shape, dtype=F32):
    return pltpu.VMEM(shape, dtype)


def local(kernel, arrays, shapes, specs=None, outs=pltpu.VMEM, **more):
    near = pl.BlockSpec(memory_space=pltpu.VMEM)
    if specs is None:
        arrays = [pltpu.with_memory_space_constraint(array, pltpu.VMEM) for array in arrays]
    return pl.pallas_call(
        kernel,
        out_shape=tuple(shapes),
        in_specs=specs or [near] * len(arrays),
        out_specs=(pl.BlockSpec(memory_space=outs),) * len(shapes),
        **more,
    )(*arrays)


def shards(tensor, run_counts, run_init, bin_init, time_init):
    rowcap, rows, width = tensor.shape
    rank = run_init.shape[1]
    flat = tensor.reshape(rowcap * rows, width)
    plane = extent(PLANE)
    half = rank // extent(PAIR)
    chunk = half // plane
    wide = width + rank

    flat = pltpu.with_memory_space_constraint(flat, pltpu.VMEM)
    runs, run_gram, empty, low, below, bins, _, times = local(
        grams_kernel,
        (bin_init, run_init, time_init, run_counts),
        (
            shape_of((rowcap, rank)),
            shape_of((rank, rank)),
            shape_of((rowcap, rank)),
            shape_of(bin_init.shape, BF16),
            shape_of((rows, rank)),
            shape_of(bin_init.shape),
            shape_of((rowcap, rank)),
            shape_of((rows, rank)),
        ),
        [pl.BlockSpec(memory_space=space) for space in (*[pl.ANY] * 3, pltpu.SMEM)],
        scratch_shapes=[pltpu.SemaphoreType.DMA((3,))],
    )
    shape = (extent(NEAR), 2 * rows, rank)
    (both,) = local(terms_kernel, (flat, low, runs, below), [shape_of(shape)])
    both = jnp.sum(exchange(both, NEAR), axis=0)
    both = exchange(jnp.broadcast_to(both[None], (extent(FAR),) + both.shape), FAR)
    other, mixed, times, time_gram = local(
        time_kernel,
        (both, times, runs, run_gram, flat),
        (shape_of((half, wide)), shape_of((half, rank)), shape_of((rows, rank)), shape_of((rank, rank))),
        scratch_shapes=[pltpu.VMEM((rank, rank), F32)],
    )
    other = swap(other)
    own, *parts = local(
        side_kernel,
        (runs, times, flat, bins),
        [shape_of((half, width))] + [shape_of((rank, width), BF16)] * 3,
    )
    (both,) = local(pair_kernel, (own, mixed, other), [shape_of((plane, chunk, wide))])
    both = exchange(both, PLANE)
    (both,) = local(spread_kernel, (both,), [shape_of((extent(FAR), chunk, wide))])
    both = exchange(both, FAR)
    (mine,) = local(bins_kernel, (both, *parts), [shape_of((plane, chunk, width))])
    mine = exchange(mine, PLANE)
    rest = swap(mine)
    own, terms = local(
        half_kernel, (mine, flat, times), (shape_of((half, width)), shape_of((rowcap, half)))
    )
    both, bins = local(
        runs_kernel,
        (terms, own, rest, flat, runs, times, time_gram),
        (shape_of((extent(TM), 2 * rowcap, rank)), shape_of((width, rank))),
        scratch_shapes=[pltpu.VMEM((rank, width), F32)],
    )
    return tuple(
        local(
            last_kernel,
            (exchange(both, TM), runs, empty, bins, times),
            [jax.ShapeDtypeStruct(shape, F32) for shape in (runs.shape, bins.shape, times.shape)],
            outs=pl.ANY,
            scratch_shapes=[pltpu.VMEM(runs.shape, F32), pltpu.SemaphoreType.DMA((3,))],
        )
    )


def solution(mesh):
    fine = Mesh(mesh.devices.reshape(tuple(SIZES.values())), tuple(SIZES))
    return jax.shard_map(
        shards,
        mesh=fine,
        in_specs=(P(RUNS, TM, None), P(RUNS), P(RUNS, None), P(), P(TM, None)),
        out_specs=(P(RUNS, None), P(), P(TM, None)),
        check_vma=False,
    )
```

```python
import jax
import jax.numpy as jnp
from jax import lax
from jax.experimental import pallas as pl
from jax.experimental.pallas import tpu as pltpu
from jax.sharding import Mesh, PartitionSpec as P

HIGH = lax.Precision.HIGHEST
F32 = jnp.float32
BF16 = jnp.bfloat16
SIZES = {"x": 4, "h": 8, "l": 2, "y": 4, "c": 2}
RUNS = ("x", "h", "l")
NEAR = ("x", "l")
FAR = ("h",)
PLANE = ("x", "l", "y")
PAIR = ("c",)
TM = ("y", "c")
FIRST = (((0,), (0,)), ((), ()))
LAST = (((1,), (1,)), ((), ()))


def exact(left, right, dims):
    return lax.dot_general(left, right, dims, precision=HIGH, preferred_element_type=F32)


def quick(left, right, dims):
    return lax.dot_general(left, right, dims, preferred_element_type=F32)


def extent(axes):
    total = 1
    for axis in axes:
        total *= SIZES[axis]
    return total


def exchange(parts, axes):
    return lax.all_to_all(parts, axes, 0, 0)


def swap(value):
    return lax.ppermute(value, PAIR, [(0, 1), (1, 0)])


def added(parts):
    total = parts[0]
    for part in range(1, parts.shape[0]):
        total += parts[part]
    return total


def terms_kernel(*refs):
    far, (both, runs_out, gram_out, empty, *near), (sems,) = refs[:5], refs[5:13], refs[13:]
    tensor, bins, run_init, times = near
    copies = [pltpu.make_async_copy(far[i], near[i], sems.at[i]) for i in range(4)]
    for copy in reversed(copies):
        copy.start()
    rowcap, rank = run_init.shape
    rows = times.shape[0]
    slot = lax.broadcasted_iota(jnp.int32, (rowcap, rank), 0)
    for copy in reversed(copies[2:]):
        copy.wait()
    live = slot < far[4][0]
    empty[...] = jnp.where(live, 0.0, 1.0)
    runs = jnp.where(live, run_init[...], 0.0)
    runs_out[...] = runs
    run_gram = exact(runs, runs, FIRST)
    gram_out[...] = run_gram
    copies[1].wait()
    full = bins[...]
    below = jnp.dot(times[...], run_gram * exact(full, full, FIRST), precision=HIGH)
    copies[0].wait()
    inner = jnp.dot(tensor[...], full.astype(BF16), preferred_element_type=F32)
    terms = runs[0:1] * inner[0:rows]
    for i in range(1, rowcap):
        terms += runs[i : i + 1] * inner[i * rows : (i + 1) * rows]
    for copy in range(both.shape[0]):
        both[copy, 0:rows] = terms
        both[copy, rows:] = below


def pieces(value):
    out = []
    for _ in range(3):
        out.append(value.astype(BF16))
        value = value - out[-1].astype(F32)
    return out


def half_terms(runs, times, tensor, side):
    half = runs.shape[1] // 2
    runs, times = runs[...], times[...]
    low = times.astype(BF16).astype(F32)
    runs = jnp.where(side == 0, runs[:, :half], runs[:, half:])
    low = jnp.where(side == 0, low[:, :half], low[:, half:])
    left = jnp.concatenate([runs[i : i + 1] * low for i in range(runs.shape[0])], axis=0)
    block = tensor[...]
    high, mid, rest = (quick(part, block, FIRST) for part in pieces(left))
    return high + mid + rest


def time_kernel(parts, times, runs, run_gram, tensor, other, mixed, times_out, gram_out, whole):
    rows = times.shape[0]
    width = tensor.shape[1]
    half = other.shape[0]
    core = lax.axis_index(PAIR)
    sums = added(parts)
    new = times[...] * sums[:rows] / sums[rows:]
    times_out[...] = new
    time_gram = exact(new, new, FIRST)
    gram_out[...] = time_gram
    whole[...] = run_gram[...] * time_gram
    mixed[...] = whole[pl.ds(core * half, half)]
    other[:, 0:width] = half_terms(runs, times_out, tensor, 1 - core)
    other[:, width:] = whole[pl.ds((1 - core) * half, half)]


def side_kernel(runs, times, tensor, bins, own, *parts):
    own[...] = half_terms(runs, times, tensor, lax.axis_index(PAIR))
    for ref, part in zip(parts, pieces(bins[...].T)):
        ref[...] = part


def pair_kernel(own, mixed, other, out):
    count, chunk, width = out.shape
    inner = own.shape[1]
    got = other[...]
    out[:, :, 0:inner] = (own[...] + got[:, :inner]).reshape(count, chunk, inner)
    out[:, :, inner:] = (mixed[...] + got[:, inner:]).reshape(count, chunk, width - inner)


def spread_kernel(parts, out):
    total = added(parts)
    for copy in range(out.shape[0]):
        out[copy] = total


def bins_kernel(parts, high, mid, low, out):
    count, chunk, width = out.shape
    rank = high.shape[0]
    start = lax.axis_index(PAIR) * (count * chunk) + lax.axis_index(PLANE) * chunk
    sums = added(parts)
    row = lax.broadcasted_iota(jnp.int32, (chunk, rank), 0) + start
    column = lax.broadcasted_iota(jnp.int32, (chunk, rank), 1)
    pick = jnp.where(column == row, 1.0, 0.0)
    split = [part.astype(F32) for part in pieces(sums[:, width:])]
    left = jnp.concatenate([*split, pick], axis=0).astype(BF16)
    first, second, third = (jnp.dot(left, ref[...], preferred_element_type=F32) for ref in (high, mid, low))
    a, b, c, d = (slice(i * chunk, (i + 1) * chunk) for i in range(4))
    below = first[a] + (first[b] + second[a]) + (first[c] + second[b] + third[a])
    mine = (first[d] + second[d] + third[d]) * sums[:, :width] / below
    for copy in range(count):
        out[copy] = mine


def half_kernel(parts, tensor, times, bins_out, terms_out):
    half, width = bins_out.shape
    rows = times.shape[0]
    core = lax.axis_index(PAIR)
    bins = parts[...].reshape(half, width)
    bins_out[...] = bins
    inner = quick(tensor[...], bins.astype(BF16), LAST)
    both = times[...]
    mine = jnp.where(core == 0, both[:, :half], both[:, half:])
    for i in range(terms_out.shape[0]):
        term = mine * inner[i * rows : (i + 1) * rows]
        terms_out[i : i + 1] = jnp.sum(term, axis=0, keepdims=True)


def runs_kernel(mine, own, parts, tensor, runs, times, time_gram, both, turned, bins_out):
    half, width = own.shape
    rowcap = runs.shape[0]
    rows = times.shape[0]
    core = lax.axis_index(PAIR)
    rest = parts[...].reshape(half, width)
    bins_out[pl.ds(core * half, half)] = own[...]
    bins_out[pl.ds((1 - core) * half, half)] = rest
    bins = bins_out[...]
    turned[...] = bins.T
    inner = quick(tensor[...], rest.astype(BF16), LAST)
    mixing = exact(bins, bins, LAST) * time_gram[...]
    below = jnp.dot(runs[...], mixing, precision=HIGH)
    full = times[...]
    side = jnp.where(core == 0, full[:, half:], full[:, :half])
    found = [
        jnp.sum(side * inner[i * rows : (i + 1) * rows], axis=0, keepdims=True)
        for i in range(rowcap)
    ]
    found = jnp.concatenate(found, axis=0)
    first = jnp.where(core == 0, mine[...], found)
    second = jnp.where(core == 0, found, mine[...])
    terms = jnp.concatenate([first, second], axis=1)
    for copy in range(both.shape[0]):
        both[copy, rowcap:] = below
        both[copy, 0:rowcap] = terms


def last_kernel(parts, runs, empty, bins, times, runs_out, bins_out, times_out, new, sems):
    copies = [
        pltpu.make_async_copy(near, far, sems.at[i])
        for i, (near, far) in enumerate(((bins, bins_out), (times, times_out), (new, runs_out)))
    ]
    copies[0].start()
    copies[1].start()
    rowcap = runs.shape[0]
    sums = added(parts)
    new[...] = runs[...] * sums[:rowcap] / (sums[rowcap:] + empty[...])
    copies[2].start()
    for copy in copies:
        copy.wait()


def shape_of(shape, dtype=F32):
    return pltpu.VMEM(shape, dtype)


def local(kernel, arrays, shapes, specs=None, outs=pltpu.VMEM, **more):
    near = pl.BlockSpec(memory_space=pltpu.VMEM)
    if specs is None:
        arrays = [pltpu.with_memory_space_constraint(array, pltpu.VMEM) for array in arrays]
    return pl.pallas_call(
        kernel,
        out_shape=tuple(shapes),
        in_specs=specs or [near] * len(arrays),
        out_specs=(pl.BlockSpec(memory_space=outs),) * len(shapes),
        **more,
    )(*arrays)


def shards(tensor, run_counts, run_init, bin_init, time_init):
    rowcap, rows, width = tensor.shape
    rank = run_init.shape[1]
    flat = tensor.reshape(rowcap * rows, width)
    plane = extent(PLANE)
    half = rank // extent(PAIR)
    chunk = half // plane
    wide = width + rank

    both, runs, run_gram, empty, flat, bins, _, times = local(
        terms_kernel,
        (flat, bin_init, run_init, time_init, run_counts),
        (
            shape_of((extent(FAR), 2 * rows, rank)),
            shape_of((rowcap, rank)),
            shape_of((rank, rank)),
            shape_of((rowcap, rank)),
            shape_of(flat.shape, flat.dtype),
            shape_of(bin_init.shape),
            shape_of((rowcap, rank)),
            shape_of((rows, rank)),
        ),
        [pl.BlockSpec(memory_space=pl.ANY)] * 4 + [pl.BlockSpec(memory_space=pltpu.SMEM)],
        scratch_shapes=[pltpu.SemaphoreType.DMA((4,))],
    )
    both = jnp.sum(exchange(both, FAR), axis=0)
    both = exchange(jnp.broadcast_to(both[None], (extent(NEAR),) + both.shape), NEAR)
    other, mixed, times, time_gram = local(
        time_kernel,
        (both, times, runs, run_gram, flat),
        (shape_of((half, wide)), shape_of((half, rank)), shape_of((rows, rank)), shape_of((rank, rank))),
        scratch_shapes=[pltpu.VMEM((rank, rank), F32)],
    )
    other = swap(other)
    own, *parts = local(
        side_kernel,
        (runs, times, flat, bins),
        [shape_of((half, width))] + [shape_of((rank, width), BF16)] * 3,
    )
    (both,) = local(pair_kernel, (own, mixed, other), [shape_of((plane, chunk, wide))])
    both = exchange(both, PLANE)
    (both,) = local(spread_kernel, (both,), [shape_of((extent(FAR), chunk, wide))])
    both = exchange(both, FAR)
    (mine,) = local(bins_kernel, (both, *parts), [shape_of((plane, chunk, width))])
    mine = exchange(mine, PLANE)
    rest = swap(mine)
    own, terms = local(
        half_kernel, (mine, flat, times), (shape_of((half, width)), shape_of((rowcap, half)))
    )
    both, bins = local(
        runs_kernel,
        (terms, own, rest, flat, runs, times, time_gram),
        (shape_of((extent(TM), 2 * rowcap, rank)), shape_of((width, rank))),
        scratch_shapes=[pltpu.VMEM((rank, width), F32)],
    )
    return tuple(
        local(
            last_kernel,
            (exchange(both, TM), runs, empty, bins, times),
            [jax.ShapeDtypeStruct(shape, F32) for shape in (runs.shape, bins.shape, times.shape)],
            outs=pl.ANY,
            scratch_shapes=[pltpu.VMEM(runs.shape, F32), pltpu.SemaphoreType.DMA((3,))],
        )
    )


def solution(mesh):
    fine = Mesh(mesh.devices.reshape(tuple(SIZES.values())), tuple(SIZES))
    return jax.shard_map(
        shards,
        mesh=fine,
        in_specs=(P(RUNS, TM, None), P(RUNS), P(RUNS, None), P(), P(TM, None)),
        out_specs=(P(RUNS, None), P(), P(TM, None)),
        check_vma=False,
    )
```

```python
import jax
import jax.numpy as jnp
from jax import lax
from jax.experimental import pallas as pl
from jax.experimental.pallas import tpu as pltpu
from jax.sharding import Mesh, PartitionSpec as P

HIGH = lax.Precision.HIGHEST
F32 = jnp.float32
BF16 = jnp.bfloat16
SIZES = {"x": 4, "h": 8, "l": 2, "y": 4, "c": 2}
RUNS = ("x", "h", "l")
NEAR = ("x", "l")
FAR = ("h",)
PLANE = ("x", "l", "y")
PAIR = ("c",)
TM = ("y", "c")
FIRST = (((0,), (0,)), ((), ()))
LAST = (((1,), (1,)), ((), ()))


def exact(left, right, dims):
    return lax.dot_general(left, right, dims, precision=HIGH, preferred_element_type=F32)


def quick(left, right, dims):
    return lax.dot_general(left, right, dims, preferred_element_type=F32)


def extent(axes):
    total = 1
    for axis in axes:
        total *= SIZES[axis]
    return total


def exchange(parts, axes):
    return lax.all_to_all(parts, axes, 0, 0)


def swap(value):
    return lax.ppermute(value, PAIR, [(0, 1), (1, 0)])


def added(parts):
    total = parts[0]
    for part in range(1, parts.shape[0]):
        total += parts[part]
    return total


def grams_kernel(*refs):
    far, count = refs[:3], refs[3]
    runs_out, gram_out, empty, low, below, *near, sems = refs[4:]
    bins, run_init, times = near
    middle = bins.shape[0] // 2
    halves = [pl.ds(i * middle, middle) for i in range(2)]
    small = [pltpu.make_async_copy(far[i], near[i], sems.at[i]) for i in (1, 2)]
    large = [
        pltpu.make_async_copy(far[0].at[part], bins.at[part], sems.at[3 * i])
        for i, part in enumerate(halves)
    ]
    for copy in (*large, *small):
        copy.start()
    slot = lax.broadcasted_iota(jnp.int32, run_init.shape, 0)
    small[0].wait()
    live = slot < count[0]
    empty[...] = jnp.where(live, 0.0, 1.0)
    runs = jnp.where(live, run_init[...], 0.0)
    runs_out[...] = runs
    run_gram = exact(runs, runs, FIRST)
    gram_out[...] = run_gram
    small[1].wait()
    grams = []
    for copy, part in zip(large, halves):
        copy.wait()
        full = bins[part]
        low[part] = full.astype(BF16)
        grams.append(square(full, FIRST))
    below[...] = jnp.dot(times[...], run_gram * (grams[0] + grams[1]), precision=HIGH)


def terms_kernel(tensor, low, runs, below, both):
    rowcap = runs.shape[0]
    rows = below.shape[0]
    inner = jnp.dot(tensor[...], low[...], preferred_element_type=F32)
    terms = runs[0:1] * inner[0:rows]
    for i in range(1, rowcap):
        terms += runs[i : i + 1] * inner[i * rows : (i + 1) * rows]
    for copy in range(both.shape[0]):
        both[copy, 0:rows] = terms
        both[copy, rows:] = below[...]


def pieces(value):
    out = []
    for _ in range(3):
        out.append(value.astype(BF16))
        value = value - out[-1].astype(F32)
    return out


def square(value, dims):
    high, mid, low = pieces(value)
    cross = quick(high, mid, dims)
    far = quick(high, low, dims)
    return quick(high, high, dims) + (cross + cross.T) + (quick(mid, mid, dims) + far + far.T)


def half_terms(runs, times, tensor, side):
    half = runs.shape[1] // 2
    runs, times = runs[...], times[...]
    low = times.astype(BF16).astype(F32)
    runs = jnp.where(side == 0, runs[:, :half], runs[:, half:])
    low = jnp.where(side == 0, low[:, :half], low[:, half:])
    left = jnp.concatenate([runs[i : i + 1] * low for i in range(runs.shape[0])], axis=0)
    block = tensor[...]
    high, mid, rest = (quick(part, block, FIRST) for part in pieces(left))
    return high + mid + rest


def time_kernel(parts, times, runs, run_gram, tensor, other, mixed, times_out, gram_out, whole):
    rows = times.shape[0]
    width = tensor.shape[1]
    half = other.shape[0]
    core = lax.axis_index(PAIR)
    sums = added(parts)
    new = times[...] * sums[:rows] / sums[rows:]
    times_out[...] = new
    time_gram = exact(new, new, FIRST)
    gram_out[...] = time_gram
    whole[...] = run_gram[...] * time_gram
    mixed[...] = whole[pl.ds(core * half, half)]
    other[:, 0:width] = half_terms(runs, times_out, tensor, 1 - core)
    other[:, width:] = whole[pl.ds((1 - core) * half, half)]


def side_kernel(runs, times, tensor, bins, own, *parts):
    own[...] = half_terms(runs, times, tensor, lax.axis_index(PAIR))
    for ref, part in zip(parts, pieces(bins[...].T)):
        ref[...] = part


def pair_kernel(own, mixed, other, out):
    count, chunk, width = out.shape
    inner = own.shape[1]
    got = other[...]
    out[:, :, 0:inner] = (own[...] + got[:, :inner]).reshape(count, chunk, inner)
    out[:, :, inner:] = (mixed[...] + got[:, inner:]).reshape(count, chunk, width - inner)


def spread_kernel(parts, out):
    total = added(parts)
    for copy in range(out.shape[0]):
        out[copy] = total


def bins_kernel(parts, high, mid, low, out):
    count, chunk, width = out.shape
    rank = high.shape[0]
    start = lax.axis_index(PAIR) * (count * chunk) + lax.axis_index(PLANE) * chunk
    sums = added(parts)
    row = lax.broadcasted_iota(jnp.int32, (chunk, rank), 0) + start
    column = lax.broadcasted_iota(jnp.int32, (chunk, rank), 1)
    pick = jnp.where(column == row, 1.0, 0.0)
    split = [part.astype(F32) for part in pieces(sums[:, width:])]
    left = jnp.concatenate([*split, pick], axis=0).astype(BF16)
    first, second, third = (jnp.dot(left, ref[...], preferred_element_type=F32) for ref in (high, mid, low))
    a, b, c, d = (slice(i * chunk, (i + 1) * chunk) for i in range(4))
    below = first[a] + (first[b] + second[a]) + (first[c] + second[b] + third[a])
    mine = (first[d] + second[d] + third[d]) * sums[:, :width] / below
    for copy in range(count):
        out[copy] = mine


def half_kernel(parts, tensor, times, bins_out, terms_out):
    half, width = bins_out.shape
    rows = times.shape[0]
    core = lax.axis_index(PAIR)
    bins = parts[...].reshape(half, width)
    bins_out[...] = bins
    inner = quick(tensor[...], bins.astype(BF16), LAST)
    both = times[...]
    mine = jnp.where(core == 0, both[:, :half], both[:, half:])
    for i in range(terms_out.shape[0]):
        term = mine * inner[i * rows : (i + 1) * rows]
        terms_out[i : i + 1] = jnp.sum(term, axis=0, keepdims=True)


def runs_kernel(mine, own, parts, tensor, runs, times, time_gram, both, turned, bins_out):
    half, width = own.shape
    rowcap = runs.shape[0]
    rows = times.shape[0]
    core = lax.axis_index(PAIR)
    rest = parts[...].reshape(half, width)
    bins_out[pl.ds(core * half, half)] = own[...]
    bins_out[pl.ds((1 - core) * half, half)] = rest
    bins = bins_out[...]
    turned[...] = bins.T
    inner = quick(tensor[...], rest.astype(BF16), LAST)
    mixing = exact(bins, bins, LAST) * time_gram[...]
    below = jnp.dot(runs[...], mixing, precision=HIGH)
    full = times[...]
    side = jnp.where(core == 0, full[:, half:], full[:, :half])
    found = [
        jnp.sum(side * inner[i * rows : (i + 1) * rows], axis=0, keepdims=True)
        for i in range(rowcap)
    ]
    found = jnp.concatenate(found, axis=0)
    first = jnp.where(core == 0, mine[...], found)
    second = jnp.where(core == 0, found, mine[...])
    terms = jnp.concatenate([first, second], axis=1)
    for copy in range(both.shape[0]):
        both[copy, rowcap:] = below
        both[copy, 0:rowcap] = terms


def last_kernel(parts, runs, empty, bins, times, runs_out, bins_out, times_out, new, sems):
    copies = [
        pltpu.make_async_copy(near, far, sems.at[i])
        for i, (near, far) in enumerate(((bins, bins_out), (times, times_out), (new, runs_out)))
    ]
    copies[0].start()
    copies[1].start()
    rowcap = runs.shape[0]
    sums = added(parts)
    new[...] = runs[...] * sums[:rowcap] / (sums[rowcap:] + empty[...])
    copies[2].start()
    for copy in copies:
        copy.wait()


def shape_of(shape, dtype=F32):
    return pltpu.VMEM(shape, dtype)


def local(kernel, arrays, shapes, specs=None, outs=pltpu.VMEM, **more):
    near = pl.BlockSpec(memory_space=pltpu.VMEM)
    if specs is None:
        arrays = [pltpu.with_memory_space_constraint(array, pltpu.VMEM) for array in arrays]
    return pl.pallas_call(
        kernel,
        out_shape=tuple(shapes),
        in_specs=specs or [near] * len(arrays),
        out_specs=(pl.BlockSpec(memory_space=outs),) * len(shapes),
        **more,
    )(*arrays)


def shards(tensor, run_counts, run_init, bin_init, time_init):
    rowcap, rows, width = tensor.shape
    rank = run_init.shape[1]
    flat = tensor.reshape(rowcap * rows, width)
    plane = extent(PLANE)
    half = rank // extent(PAIR)
    chunk = half // plane
    wide = width + rank

    flat = pltpu.with_memory_space_constraint(flat, pltpu.VMEM)
    runs, run_gram, empty, low, below, bins, _, times = local(
        grams_kernel,
        (bin_init, run_init, time_init, run_counts),
        (
            shape_of((rowcap, rank)),
            shape_of((rank, rank)),
            shape_of((rowcap, rank)),
            shape_of(bin_init.shape, BF16),
            shape_of((rows, rank)),
            shape_of(bin_init.shape),
            shape_of((rowcap, rank)),
            shape_of((rows, rank)),
        ),
        [pl.BlockSpec(memory_space=space) for space in (*[pl.ANY] * 3, pltpu.SMEM)],
        scratch_shapes=[pltpu.SemaphoreType.DMA((4,))],
    )
    shape = (extent(NEAR), 2 * rows, rank)
    (both,) = local(terms_kernel, (flat, low, runs, below), [shape_of(shape)])
    both = jnp.sum(exchange(both, NEAR), axis=0)
    both = exchange(jnp.broadcast_to(both[None], (extent(FAR),) + both.shape), FAR)
    other, mixed, times, time_gram = local(
        time_kernel,
        (both, times, runs, run_gram, flat),
        (shape_of((half, wide)), shape_of((half, rank)), shape_of((rows, rank)), shape_of((rank, rank))),
        scratch_shapes=[pltpu.VMEM((rank, rank), F32)],
    )
    other = swap(other)
    own, *parts = local(
        side_kernel,
        (runs, times, flat, bins),
        [shape_of((half, width))] + [shape_of((rank, width), BF16)] * 3,
    )
    (both,) = local(pair_kernel, (own, mixed, other), [shape_of((plane, chunk, wide))])
    both = exchange(both, PLANE)
    (both,) = local(spread_kernel, (both,), [shape_of((extent(FAR), chunk, wide))])
    both = exchange(both, FAR)
    (mine,) = local(bins_kernel, (both, *parts), [shape_of((plane, chunk, width))])
    mine = exchange(mine, PLANE)
    rest = swap(mine)
    own, terms = local(
        half_kernel, (mine, flat, times), (shape_of((half, width)), shape_of((rowcap, half)))
    )
    both, bins = local(
        runs_kernel,
        (terms, own, rest, flat, runs, times, time_gram),
        (shape_of((extent(TM), 2 * rowcap, rank)), shape_of((width, rank))),
        scratch_shapes=[pltpu.VMEM((rank, width), F32)],
    )
    return tuple(
        local(
            last_kernel,
            (exchange(both, TM), runs, empty, bins, times),
            [jax.ShapeDtypeStruct(shape, F32) for shape in (runs.shape, bins.shape, times.shape)],
            outs=pl.ANY,
            scratch_shapes=[pltpu.VMEM(runs.shape, F32), pltpu.SemaphoreType.DMA((3,))],
        )
    )


def solution(mesh):
    fine = Mesh(mesh.devices.reshape(tuple(SIZES.values())), tuple(SIZES))
    return jax.shard_map(
        shards,
        mesh=fine,
        in_specs=(P(RUNS, TM, None), P(RUNS), P(RUNS, None), P(), P(TM, None)),
        out_specs=(P(RUNS, None), P(), P(TM, None)),
        check_vma=False,
    )
```

```python
import jax
import jax.numpy as jnp
from jax import lax
from jax.experimental import pallas as pl
from jax.experimental.pallas import tpu as pltpu
from jax.sharding import Mesh, PartitionSpec as P

HIGH = lax.Precision.HIGHEST
F32 = jnp.float32
BF16 = jnp.bfloat16
SIZES = {"x": 4, "h": 8, "l": 2, "y": 4, "c": 2}
RUNS = ("x", "h", "l")
NEAR = ("x", "l")
FAR = ("h",)
PLANE = ("x", "l", "y")
PAIR = ("c",)
TM = ("y", "c")
FIRST = (((0,), (0,)), ((), ()))
LAST = (((1,), (1,)), ((), ()))


def exact(left, right, dims):
    return lax.dot_general(left, right, dims, precision=HIGH, preferred_element_type=F32)


def quick(left, right, dims):
    return lax.dot_general(left, right, dims, preferred_element_type=F32)


def extent(axes):
    total = 1
    for axis in axes:
        total *= SIZES[axis]
    return total


def exchange(parts, axes):
    return lax.all_to_all(parts, axes, 0, 0)


def swap(value):
    return lax.ppermute(value, PAIR, [(0, 1), (1, 0)])


def added(parts):
    total = parts[0]
    for part in range(1, parts.shape[0]):
        total += parts[part]
    return total


def terms_kernel(*refs):
    far, (both, runs_out, gram_out, empty, *near), (sems,) = refs[:5], refs[5:13], refs[13:]
    tensor, bins, run_init, times = near
    copies = [pltpu.make_async_copy(far[i], near[i], sems.at[i]) for i in range(4)]
    for copy in reversed(copies):
        copy.start()
    rowcap, rank = run_init.shape
    rows = times.shape[0]
    slot = lax.broadcasted_iota(jnp.int32, (rowcap, rank), 0)
    for copy in reversed(copies[2:]):
        copy.wait()
    live = slot < far[4][0]
    empty[...] = jnp.where(live, 0.0, 1.0)
    runs = jnp.where(live, run_init[...], 0.0)
    runs_out[...] = runs
    run_gram = exact(runs, runs, FIRST)
    gram_out[...] = run_gram
    copies[1].wait()
    full = bins[...]
    below = jnp.dot(times[...], run_gram * square(full, FIRST), precision=HIGH)
    copies[0].wait()
    inner = jnp.dot(tensor[...], full.astype(BF16), preferred_element_type=F32)
    terms = runs[0:1] * inner[0:rows]
    for i in range(1, rowcap):
        terms += runs[i : i + 1] * inner[i * rows : (i + 1) * rows]
    for copy in range(both.shape[0]):
        both[copy, 0:rows] = terms
        both[copy, rows:] = below


def pieces(value):
    out = []
    for _ in range(3):
        out.append(value.astype(BF16))
        value = value - out[-1].astype(F32)
    return out


def square(value, dims):
    high, mid, low = pieces(value)
    cross = quick(high, mid, dims)
    far = quick(high, low, dims)
    return quick(high, high, dims) + (cross + cross.T) + (quick(mid, mid, dims) + far + far.T)


def half_terms(runs, times, tensor, side):
    half = runs.shape[1] // 2
    runs, times = runs[...], times[...]
    low = times.astype(BF16).astype(F32)
    runs = jnp.where(side == 0, runs[:, :half], runs[:, half:])
    low = jnp.where(side == 0, low[:, :half], low[:, half:])
    left = jnp.concatenate([runs[i : i + 1] * low for i in range(runs.shape[0])], axis=0)
    block = tensor[...]
    high, mid, rest = (quick(part, block, FIRST) for part in pieces(left))
    return high + mid + rest


def time_kernel(parts, times, runs, run_gram, tensor, other, mixed, times_out, gram_out, whole):
    rows = times.shape[0]
    width = tensor.shape[1]
    half = other.shape[0]
    core = lax.axis_index(PAIR)
    sums = added(parts)
    new = times[...] * sums[:rows] / sums[rows:]
    times_out[...] = new
    time_gram = exact(new, new, FIRST)
    gram_out[...] = time_gram
    whole[...] = run_gram[...] * time_gram
    mixed[...] = whole[pl.ds(core * half, half)]
    other[:, 0:width] = half_terms(runs, times_out, tensor, 1 - core)
    other[:, width:] = whole[pl.ds((1 - core) * half, half)]


def side_kernel(runs, times, tensor, bins, own, *parts):
    own[...] = half_terms(runs, times, tensor, lax.axis_index(PAIR))
    for ref, part in zip(parts, pieces(bins[...].T)):
        ref[...] = part


def pair_kernel(own, mixed, other, out):
    count, chunk, width = out.shape
    inner = own.shape[1]
    got = other[...]
    out[:, :, 0:inner] = (own[...] + got[:, :inner]).reshape(count, chunk, inner)
    out[:, :, inner:] = (mixed[...] + got[:, inner:]).reshape(count, chunk, width - inner)


def spread_kernel(parts, out):
    total = added(parts)
    for copy in range(out.shape[0]):
        out[copy] = total


def bins_kernel(parts, high, mid, low, out):
    count, chunk, width = out.shape
    rank = high.shape[0]
    start = lax.axis_index(PAIR) * (count * chunk) + lax.axis_index(PLANE) * chunk
    sums = added(parts)
    row = lax.broadcasted_iota(jnp.int32, (chunk, rank), 0) + start
    column = lax.broadcasted_iota(jnp.int32, (chunk, rank), 1)
    pick = jnp.where(column == row, 1.0, 0.0)
    split = [part.astype(F32) for part in pieces(sums[:, width:])]
    left = jnp.concatenate([*split, pick], axis=0).astype(BF16)
    first, second, third = (jnp.dot(left, ref[...], preferred_element_type=F32) for ref in (high, mid, low))
    a, b, c, d = (slice(i * chunk, (i + 1) * chunk) for i in range(4))
    below = first[a] + (first[b] + second[a]) + (first[c] + second[b] + third[a])
    mine = (first[d] + second[d] + third[d]) * sums[:, :width] / below
    for copy in range(count):
        out[copy] = mine


def half_kernel(parts, tensor, times, bins_out, terms_out):
    half, width = bins_out.shape
    rows = times.shape[0]
    core = lax.axis_index(PAIR)
    bins = parts[...].reshape(half, width)
    bins_out[...] = bins
    inner = quick(tensor[...], bins.astype(BF16), LAST)
    both = times[...]
    mine = jnp.where(core == 0, both[:, :half], both[:, half:])
    for i in range(terms_out.shape[0]):
        term = mine * inner[i * rows : (i + 1) * rows]
        terms_out[i : i + 1] = jnp.sum(term, axis=0, keepdims=True)


def runs_kernel(mine, own, parts, tensor, runs, times, time_gram, both, turned, bins_out):
    half, width = own.shape
    rowcap = runs.shape[0]
    rows = times.shape[0]
    core = lax.axis_index(PAIR)
    rest = parts[...].reshape(half, width)
    bins_out[pl.ds(core * half, half)] = own[...]
    bins_out[pl.ds((1 - core) * half, half)] = rest
    bins = bins_out[...]
    turned[...] = bins.T
    inner = quick(tensor[...], rest.astype(BF16), LAST)
    mixing = exact(bins, bins, LAST) * time_gram[...]
    below = jnp.dot(runs[...], mixing, precision=HIGH)
    full = times[...]
    side = jnp.where(core == 0, full[:, half:], full[:, :half])
    found = [
        jnp.sum(side * inner[i * rows : (i + 1) * rows], axis=0, keepdims=True)
        for i in range(rowcap)
    ]
    found = jnp.concatenate(found, axis=0)
    first = jnp.where(core == 0, mine[...], found)
    second = jnp.where(core == 0, found, mine[...])
    terms = jnp.concatenate([first, second], axis=1)
    for copy in range(both.shape[0]):
        both[copy, rowcap:] = below
        both[copy, 0:rowcap] = terms


def last_kernel(parts, runs, empty, bins, times, runs_out, bins_out, times_out, new, sems):
    copies = [
        pltpu.make_async_copy(near, far, sems.at[i])
        for i, (near, far) in enumerate(((bins, bins_out), (times, times_out), (new, runs_out)))
    ]
    copies[0].start()
    copies[1].start()
    rowcap = runs.shape[0]
    sums = added(parts)
    new[...] = runs[...] * sums[:rowcap] / (sums[rowcap:] + empty[...])
    copies[2].start()
    for copy in copies:
        copy.wait()


def shape_of(shape, dtype=F32):
    return pltpu.VMEM(shape, dtype)


def local(kernel, arrays, shapes, specs=None, outs=pltpu.VMEM, **more):
    near = pl.BlockSpec(memory_space=pltpu.VMEM)
    if specs is None:
        arrays = [pltpu.with_memory_space_constraint(array, pltpu.VMEM) for array in arrays]
    return pl.pallas_call(
        kernel,
        out_shape=tuple(shapes),
        in_specs=specs or [near] * len(arrays),
        out_specs=(pl.BlockSpec(memory_space=outs),) * len(shapes),
        **more,
    )(*arrays)


def shards(tensor, run_counts, run_init, bin_init, time_init):
    rowcap, rows, width = tensor.shape
    rank = run_init.shape[1]
    flat = tensor.reshape(rowcap * rows, width)
    plane = extent(PLANE)
    half = rank // extent(PAIR)
    chunk = half // plane
    wide = width + rank

    both, runs, run_gram, empty, flat, bins, _, times = local(
        terms_kernel,
        (flat, bin_init, run_init, time_init, run_counts),
        (
            shape_of((extent(NEAR), 2 * rows, rank)),
            shape_of((rowcap, rank)),
            shape_of((rank, rank)),
            shape_of((rowcap, rank)),
            shape_of(flat.shape, flat.dtype),
            shape_of(bin_init.shape),
            shape_of((rowcap, rank)),
            shape_of((rows, rank)),
        ),
        [pl.BlockSpec(memory_space=pl.ANY)] * 4 + [pl.BlockSpec(memory_space=pltpu.SMEM)],
        scratch_shapes=[pltpu.SemaphoreType.DMA((4,))],
    )
    both = jnp.sum(exchange(both, NEAR), axis=0)
    both = exchange(jnp.broadcast_to(both[None], (extent(FAR),) + both.shape), FAR)
    other, mixed, times, time_gram = local(
        time_kernel,
        (both, times, runs, run_gram, flat),
        (shape_of((half, wide)), shape_of((half, rank)), shape_of((rows, rank)), shape_of((rank, rank))),
        scratch_shapes=[pltpu.VMEM((rank, rank), F32)],
    )
    other = swap(other)
    own, *parts = local(
        side_kernel,
        (runs, times, flat, bins),
        [shape_of((half, width))] + [shape_of((rank, width), BF16)] * 3,
    )
    (both,) = local(pair_kernel, (own, mixed, other), [shape_of((plane, chunk, wide))])
    both = exchange(both, PLANE)
    (both,) = local(spread_kernel, (both,), [shape_of((extent(FAR), chunk, wide))])
    both = exchange(both, FAR)
    (mine,) = local(bins_kernel, (both, *parts), [shape_of((plane, chunk, width))])
    mine = exchange(mine, PLANE)
    rest = swap(mine)
    own, terms = local(
        half_kernel, (mine, flat, times), (shape_of((half, width)), shape_of((rowcap, half)))
    )
    both, bins = local(
        runs_kernel,
        (terms, own, rest, flat, runs, times, time_gram),
        (shape_of((extent(TM), 2 * rowcap, rank)), shape_of((width, rank))),
        scratch_shapes=[pltpu.VMEM((rank, width), F32)],
    )
    return tuple(
        local(
            last_kernel,
            (exchange(both, TM), runs, empty, bins, times),
            [jax.ShapeDtypeStruct(shape, F32) for shape in (runs.shape, bins.shape, times.shape)],
            outs=pl.ANY,
            scratch_shapes=[pltpu.VMEM(runs.shape, F32), pltpu.SemaphoreType.DMA((3,))],
        )
    )


def solution(mesh):
    fine = Mesh(mesh.devices.reshape(tuple(SIZES.values())), tuple(SIZES))
    return jax.shard_map(
        shards,
        mesh=fine,
        in_specs=(P(RUNS, TM, None), P(RUNS), P(RUNS, None), P(), P(TM, None)),
        out_specs=(P(RUNS, None), P(), P(TM, None)),
        check_vma=False,
    )
```
